256 devices in a mesh: row: 32 (over z, y), col: 8 (over x, core).
Axes of the slice: x: 4, y: 4, z: 8, core: 2. Of those that a mesh axis runs over, the one named last changes fastest.
Arguments:
- edit_keys: bfloat16 [256, 14336], P('row', 'col'), may hold values from -6.75 to 6.75
- edit_shifts: bfloat16 [256, 4096], P('row', 'col'), may hold values from -6 to 6
- ridge_scale: float32 [1], replicated, may hold values from 0.5 to 2
Outputs:
- panel_a: float32 [14336, 256], P('row')
- panel_b: float32 [14336, 256], P('row')
- trailing: float32 [14336, 14336], P('row', 'col')
- forward: float32 [14336, 4096], P('row', 'col')
The draws below stay inside these ranges and needn't reach their ends.
All inputs are finite; a program needn't handle non-finite values.
Results may differ from the reference program's by a relative error of at most 0.0003.
Values may be sent and summed in bfloat16 or wider, within the bound.
A program may use at most 64 MiB of HBM per device.

```python
import math
import jax
import jax.numpy as jnp
from jax import lax

UNITS = 14336
OUT_WIDTH = 4096
KEY_ROWS = 256
PANEL = 256
N_COL = 8


def draw_edit_keys(key, part):
    draw_one = jax.random.fold_in(jax.random.fold_in(key, 11), 0)
    draw_two = jax.random.fold_in(jax.random.fold_in(key, 11), 1)
    draw_three = jax.random.fold_in(jax.random.fold_in(key, 11), 2)
    draw_five = jax.random.fold_in(jax.random.fold_in(key, 11), 4)
    draw_six = jax.random.fold_in(jax.random.fold_in(key, 11), 5)
    draw_seven = jax.random.fold_in(jax.random.fold_in(key, 11), 6)
    trend_rows = 3.0 ** (0.5 * jnp.arange(KEY_ROWS, dtype=jnp.float32) / KEY_ROWS)
    trend_units = 3.0 ** (0.5 * jnp.arange(UNITS, dtype=jnp.float32) / UNITS)
    unit_ids = jnp.arange(UNITS, dtype=jnp.int32)
    start_b = UNITS // N_COL
    loud_units = (unit_ids < PANEL) | (unit_ids >= start_b) & (unit_ids < start_b + PANEL)
    shared_rows = jnp.clip(jax.random.normal(draw_five, (KEY_ROWS, 1), jnp.float32), -2.5, 2.5)
    signs = jnp.where(jax.random.normal(draw_seven, (1, UNITS), jnp.float32) < 0.0, -1.0, 1.0)
    unit_weights = jax.random.uniform(draw_six, (1, UNITS), jnp.float32, 0.6, 1.3) * signs
    noise = jnp.clip(jax.random.normal(draw_one, (KEY_ROWS, UNITS), jnp.float32), -4.0, 4.0)
    quiet_values = noise
    low_end = 0.3
    loud_values = jnp.clip(shared_rows * unit_weights + 0.35 * noise, -4.0, 4.0)
    base_values = jnp.where(loud_units[None, :], loud_values, 0.25 * quiet_values)
    row_scale = jnp.exp(jax.random.uniform(draw_two, (KEY_ROWS,), jnp.float32, math.log(low_end), math.log(3.0)))
    unit_scale = jnp.exp(jax.random.uniform(draw_three, (UNITS,), jnp.float32, math.log(low_end), math.log(3.0)))
    scaled = base_values * (row_scale * trend_rows)[:, None] * (unit_scale * trend_units)[None, :]
    return (scaled / math.sqrt(KEY_ROWS)).astype(jnp.bfloat16)


def steps_of(rng, shape, cuts, smallest, top_value):
    factor_of, own = 1.0, jax.random.fold_in(rng, 6)
    for position, blocks in cuts:
        heights = jnp.exp(jax.random.uniform(jax.random.fold_in(own, position), (blocks,), jnp.float32, smallest / len(cuts), top_value / len(cuts)))
        factor_of = factor_of * jnp.repeat(heights, shape[position] // blocks).reshape([-1 if axis == position else 1 for axis in range(len(shape))])
    return factor_of


def centred(rng, extent, width, most, shards=(), held_as=jnp.bfloat16):
    entries = width * jax.random.normal(rng, extent, jnp.float32)
    if shards:
        entries = entries * steps_of(rng, extent, shards, -0.22, 0.18)
    return jnp.clip(entries, -most, most).astype(held_as)


def setup_inputs(seed: int = 0) -> dict:
    seeds = jax.random.split(jax.random.key(seed), 4)
    return {
        "edit_keys": draw_edit_keys(jax.random.fold_in(seeds[3], 71), 0),
        "edit_shifts": centred(seeds[1], (KEY_ROWS, OUT_WIDTH), 1.0, 6.0, ((0, 32), (1, 8))),
        "ridge_scale": jnp.clip(jnp.exp(jax.random.uniform(seeds[2], (1,), jnp.float32, math.log(0.5), math.log(2.0))), 0.5, 2.0),
    }


def reference(edit_keys, edit_shifts, ridge_scale):
    widened = edit_keys.astype(jnp.float32)
    amount = ridge_scale[0] * jnp.sum(widened * widened) / UNITS
    gram = jnp.dot(edit_keys.T.astype(jnp.float32), edit_keys.astype(jnp.float32), preferred_element_type=jnp.float32)
    diagonal_ids = jnp.arange(UNITS, dtype=jnp.int32)
    gram = gram.at[diagonal_ids, diagonal_ids].add(amount)
    rhs_full = jnp.dot(edit_keys.T.astype(jnp.float32), edit_shifts.astype(jnp.float32), preferred_element_type=jnp.float32)
    start_b = UNITS // N_COL
    lower_a = jnp.linalg.cholesky(gram[:PANEL, :PANEL])
    panel_a = jax.scipy.linalg.solve_triangular(lower_a, gram[:, :PANEL].T, lower=True).T
    panel_a = panel_a.at[:PANEL].set(lower_a)
    solved_a = jax.scipy.linalg.solve_triangular(lower_a, rhs_full[:PANEL], lower=True)
    column_b = gram[:, start_b:start_b + PANEL] - jnp.dot(panel_a, panel_a[start_b:start_b + PANEL].T, precision=lax.Precision.HIGHEST)
    lower_b = jnp.linalg.cholesky(column_b[start_b:start_b + PANEL])
    panel_b = jax.scipy.linalg.solve_triangular(lower_b, column_b.T, lower=True).T
    panel_b = panel_b.at[:PANEL].set(0.0).at[start_b:start_b + PANEL].set(lower_b)
    rhs_one = rhs_full - jnp.dot(panel_a, solved_a, precision=lax.Precision.HIGHEST)
    solved_b = jax.scipy.linalg.solve_triangular(lower_b, rhs_one[start_b:start_b + PANEL], lower=True)
    rhs_two = rhs_one - jnp.dot(panel_b, solved_b, precision=lax.Precision.HIGHEST)
    both_panels = jnp.concatenate([panel_a, panel_b], axis=1)
    trailing = gram - jnp.dot(both_panels, both_panels.T, precision=lax.Precision.HIGHEST)
    dropped = (diagonal_ids < PANEL) | (diagonal_ids >= start_b) & (diagonal_ids < start_b + PANEL)
    trailing = jnp.where(dropped[:, None] | dropped[None, :], 0.0, trailing)
    forward = rhs_two.at[:PANEL].set(solved_a).at[start_b:start_b + PANEL].set(solved_b)
    return (panel_a, panel_b, trailing, forward)
```

```python
import functools

import jax
import jax.numpy as jnp
from jax import lax
from jax.experimental import pallas as pl
from jax.experimental.pallas import tpu as pltpu
from jax.sharding import PartitionSpec as P

F32, BF16 = jnp.float32, jnp.bfloat16
PANEL = 256
ROWS, COLS, YS = 32, 8, 4
ZS = ROWS // YS
SLAB = 8
UNITS = 14336
COL_UNITS = UNITS // COLS
ROW_UNITS = UNITS // ROWS
SHIFTS = 512
WIDE = COL_UNITS + SHIFTS
WIN = 512
KEYS = 256
MESH = pl.DeviceIdType.MESH


def split2(x):
    high = x.astype(BF16)
    return high, (x - high.astype(F32)).astype(BF16)


def split3(x):
    high = x.astype(BF16)
    rest = x - high.astype(F32)
    mid = rest.astype(BF16)
    return high, mid, (rest - mid.astype(F32)).astype(BF16)


def mm(a, b):
    return jnp.dot(a, b, preferred_element_type=F32)


def mm_nt(a, b):
    return lax.dot_general(a, b, (((1,), (1,)), ((), ())), preferred_element_type=F32)


def remote(src, dst, send, recv, row, col):
    return pltpu.make_async_remote_copy(
        src_ref=src, dst_ref=dst, send_sem=send, recv_sem=recv, device_id=(row, col), device_id_type=MESH
    )


def window_start(y):
    return y * ROW_UNITS - 64 * lax.rem(y, 2)


def exchange_kernel(
    keys, shifts, crit, sums, wide, window, own_sum, col_sums,
    s_local, s_send1, r_sum1, r_crit1, s_send2, r_sum2, r_crit2, s_y, r_y, s_z, r_z, s_w, r_w,
):
    row, col = lax.axis_index("row"), lax.axis_index("col")
    z, y = row // YS, lax.rem(row, YS)

    barrier = pltpu.get_barrier_semaphore()

    def greet_row(i, carry):
        pl.semaphore_signal(barrier, inc=1, device_id=(lax.rem(row + i, ROWS), col), device_id_type=MESH)
        return carry

    def greet_col(i, carry):
        pl.semaphore_signal(barrier, inc=1, device_id=(row, lax.rem(col + i, COLS)), device_id_type=MESH)
        return carry

    lax.fori_loop(1, COLS, greet_col, 0)
    lax.fori_loop(1, ROWS, greet_row, 0)

    k32 = keys[...].astype(F32)
    sq = k32 * k32
    part = sq[:, 0:128]
    for t in range(1, COL_UNITS // 128):
        part = part + sq[:, 128 * t : 128 * (t + 1)]
    own_sum[0] = jnp.sum(part, axis=0, keepdims=True)

    local = [
        pltpu.make_async_copy(keys, wide.at[row, :, pl.ds(0, COL_UNITS)], s_local.at[0]),
        pltpu.make_async_copy(shifts, wide.at[row, :, pl.ds(COL_UNITS, SHIFTS)], s_local.at[1]),
        pltpu.make_async_copy(own_sum.at[0], col_sums.at[col], s_local.at[2]),
    ]
    for copy in local:
        copy.start()

    for half in range(2):

        @pl.when(col == half)
        def _():
            copy = pltpu.make_async_copy(
                keys.at[:, pl.ds(0, PANEL)], crit.at[row, :, pl.ds(half * PANEL, PANEL)], s_local.at[3]
            )
            copy.start()
            copy.wait()

    @pl.when(z == col)
    def _():
        for yy in range(YS):
            start = yy * ROW_UNITS - 64 * (yy % 2)

            @pl.when(y == yy)
            def _():
                copy = pltpu.make_async_copy(keys.at[:, pl.ds(start, WIN)], window.at[row], s_local.at[3])
                copy.start()
                copy.wait()

    pl.semaphore_wait(barrier, ROWS + COLS - 2)

    def send_sum1(i, carry):
        remote(own_sum.at[0], col_sums.at[col], s_send1.at[0], r_sum1, row, lax.rem(col + i, COLS)).start()
        return carry

    for half in range(2):

        @pl.when(col == half)
        def _():
            def send_crit1(i, carry):
                remote(
                    keys.at[:, pl.ds(0, PANEL)],
                    crit.at[row, :, pl.ds(half * PANEL, PANEL)],
                    s_send1.at[1],
                    r_crit1.at[half],
                    row,
                    lax.rem(col + i, COLS),
                ).start()
                return carry

            lax.fori_loop(1, COLS, send_crit1, 0)

    lax.fori_loop(1, COLS, send_sum1, 0)
    for copy in local:
        copy.wait()
    pltpu.make_async_copy(col_sums.at[pl.ds(0, COLS - 1)], col_sums.at[pl.ds(0, COLS - 1)], r_sum1).wait()
    for half in range(2):

        @pl.when(col != half)
        def _():
            ref = crit.at[row, :, pl.ds(half * PANEL, PANEL)]
            pltpu.make_async_copy(ref, ref, r_crit1.at[half]).wait()

    def send2(i, carry):
        peer = lax.rem(row + i, ROWS)
        remote(crit.at[row], crit.at[row], s_send2.at[0], r_crit2, peer, col).start()
        remote(col_sums, sums.at[row], s_send2.at[1], r_sum2, peer, col).start()
        return carry

    lax.fori_loop(1, ROWS, send2, 0)
    copy = pltpu.make_async_copy(col_sums, sums.at[row], s_local.at[3])
    copy.start()
    copy.wait()

    def await_bytes(ref, sem):
        pltpu.make_async_copy(ref, ref, sem).wait()

    await_bytes(crit.at[pl.ds(0, ROWS - 1)], r_crit2)
    await_bytes(sums.at[pl.ds(0, ROWS - 1)], r_sum2)

    def send_y(i, carry):
        peer = z * YS + lax.rem(y + i, YS)
        remote(wide.at[row], wide.at[row], s_y, r_y, peer, col).start()
        return carry

    lax.fori_loop(1, YS, send_y, 0)

    def send_window(yy):
        start = yy * ROW_UNITS - 64 * (yy % 2)
        target = col * YS + yy

        def body(i, carry):
            @pl.when((target != row) | (i != col))
            def _():
                remote(keys.at[:, pl.ds(start, WIN)], window.at[row], s_w, r_w, target, i).start()

            return carry

        lax.fori_loop(0, COLS, body, 0)

    for yy in range(YS):
        send_window(yy)

    await_bytes(wide.at[pl.ds(0, YS - 1)], r_y)

    up = lax.rem(z + 1, ZS) * YS + y
    down = lax.rem(z + ZS - 1, ZS) * YS + y
    for step in range(4):
        from_below = lax.rem(z + ZS - step, ZS) * YS
        from_above = lax.rem(z + step, ZS) * YS
        count = YS if step < 3 else YS // 2
        ref = wide.at[pl.ds(from_below, count)]
        remote(ref, ref, s_z.at[0, step], r_z.at[0, step], up, col).start()
        ref = wide.at[pl.ds(from_above + YS - count, count)]
        remote(ref, ref, s_z.at[1, step], r_z.at[1, step], down, col).start()
        await_bytes(wide.at[pl.ds(0, count)], r_z.at[0, step])
        await_bytes(wide.at[pl.ds(0, count)], r_z.at[1, step])

    @pl.when(z == col)
    def _():
        await_bytes(window.at[pl.ds(0, ROWS - 1)], r_w)

    @pl.when(z != col)
    def _():
        await_bytes(window, r_w)

    await_bytes(col_sums.at[pl.ds(0, COLS - 1)], s_send1.at[0])

    @pl.when(col < 2)
    def _():
        await_bytes(crit.at[pl.ds(0, COLS - 1), :, pl.ds(0, PANEL)], s_send1.at[1])

    await_bytes(crit.at[pl.ds(0, ROWS - 1)], s_send2.at[0])
    await_bytes(sums.at[pl.ds(0, ROWS - 1)], s_send2.at[1])
    await_bytes(wide.at[pl.ds(0, YS - 1)], s_y)

    @pl.when(row // YS == col)
    def _():
        await_bytes(window.at[pl.ds(0, ROWS - 1)], s_w)

    @pl.when(row // YS != col)
    def _():
        await_bytes(window, s_w)

    for step in range(4):
        count = YS if step < 3 else YS // 2
        for way in range(2):
            await_bytes(wide.at[pl.ds(0, count)], s_z.at[way, step])


def exchange(keys, shifts):
    dma = pltpu.SemaphoreType.DMA
    vmem = pl.BlockSpec(memory_space=pltpu.VMEM)
    return pl.pallas_call(
        exchange_kernel,
        out_shape=(
            jax.ShapeDtypeStruct((ROWS, SLAB, 2 * PANEL), BF16),
            jax.ShapeDtypeStruct((ROWS, COLS, 1, 128), F32),
            jax.ShapeDtypeStruct((ROWS, SLAB, WIDE), BF16),
            jax.ShapeDtypeStruct((ROWS, SLAB, WIN), BF16),
        ),
        in_specs=[vmem, vmem],
        out_specs=(vmem, vmem, vmem, vmem),
        scratch_shapes=[
            pltpu.VMEM((1, 1, 128), F32),
            pltpu.VMEM((COLS, 1, 128), F32),
            dma((4,)), dma((2,)), dma, dma((2,)), dma((2,)), dma, dma, dma, dma, dma((2, 4)), dma((2, 4)), dma, dma,
        ],
        compiler_params=pltpu.CompilerParams(collective_id=0, has_side_effects=True),
        name="exchange",
    )(keys, shifts)


def row_bcast(v, k):
    return jnp.broadcast_to(v[k : k + 1, :], (8, v.shape[1]))


def factor16(R, base, s, j, nt, diag_next):
    o = 16 * j
    iota = lax.broadcasted_iota(jnp.int32, (8, 128), 0)
    last = j == 7
    ng = 2 if last else 4
    lanes = slice(128 * s, 128 * s + 128)
    T = list(diag_next) if diag_next is not None else [R[base + 8 * g : base + 8 * g + 8, lanes] for g in range(2)]
    for g in range(2, ng):
        T.append(R[base + 8 * g : base + 8 * g + 8, lanes])
    C = [[None] * 4 for _ in range(16)]
    for k in range(16):
        for g in range(k // 8, ng):
            C[k][g] = jnp.broadcast_to(T[g][:, o + k : o + k + 1], (8, 128))
    Y = {t: [R[base + 8 * g : base + 8 * g + 8, 128 * t : 128 * t + 128] for g in range(2)] for t in range(s + 1, nt)}
    rv = [jnp.zeros((8, 128), F32)] * 2
    for k in range(16):
        gk, kk = k // 8, k % 8
        p = row_bcast(C[k][gk], kk)
        rp = 1.0 / p
        rv[gk] = jnp.where(iota == kk, lax.rsqrt(p), rv[gk])
        M = [None] * 4
        for g in range(gk, ng):
            M[g] = C[k][g] * rp
        for jj in range(k + 1, 16):
            c = row_bcast(C[k][jj // 8], jj % 8)
            for g in range(jj // 8, ng):
                C[jj][g] = C[jj][g] - M[g] * c
        M[gk] = None if kk == 7 else jnp.where(iota > kk, M[gk], 0.0)
        yk = row_bcast(T[gk], kk)
        for g in range(gk, ng):
            if M[g] is not None:
                T[g] = T[g] - M[g] * yk
        for t in range(s + 1, nt):
            yk = row_bcast(Y[t][gk], kk)
            for g in range(gk, 2):
                if M[g] is not None:
                    Y[t][g] = Y[t][g] - M[g] * yk
    U = {s: jnp.concatenate([T[0] * rv[0], T[1] * rv[1]], axis=0)}
    for t in range(s + 1, nt):
        U[t] = jnp.concatenate([Y[t][0] * rv[0], Y[t][1] * rv[1]], axis=0)
    for t in range(s, nt):
        R[base : base + 16, 128 * t : 128 * t + 128] = U[t]
    if last:
        return None
    zero = jnp.zeros((16, 128), BF16)
    parts = {t: split3(U[t]) for t in range(s, nt)}
    h, m, l = parts[s]
    left = jnp.concatenate([h, h, m, h, l, m, zero, zero], axis=0)
    left = jnp.transpose(left.astype(F32)).astype(BF16)[16 * (j + 1) :, :]
    below = 16 * (7 - j)
    for t in range(s, nt):
        h, m, l = parts[t]
        right = jnp.concatenate([h, m, h, l, h, m, zero, zero], axis=0)
        if t == s:
            if below > 16:
                R[base + 32 : base + 16 + below, lanes] -= mm(left[16:], right)
        else:
            R[base + 16 : base + 16 + below, 128 * t : 128 * t + 128] -= mm(left, right)
    return T[2], T[3]


def factor_kernel(ridge, kp_ref, sums_ref, u_ref, m_ref, amount_ref):
    nsuper = 4
    n = 2 * PANEL
    nt = nsuper + 2
    R = u_ref
    total = jnp.sum(jnp.sum(sums_ref[...], axis=0, keepdims=True), axis=1, keepdims=True)
    amount = ridge[0] * total / UNITS
    amount_ref[...] = jnp.broadcast_to(amount, (8, 128))
    kp = kp_ref[...]
    kpt = jnp.transpose(kp.astype(F32))
    R[:, n:] = kpt
    kptb = kpt.astype(BF16)
    i0 = lax.broadcasted_iota(jnp.int32, (128, 128), 0)
    i1 = lax.broadcasted_iota(jnp.int32, (128, 128), 1)
    for s in range(nsuper):
        rows = slice(128 * s, 128 * s + 128)
        R[rows, 128 * s : n] = mm(kptb[rows, :], kp[:, 128 * s :])
        R[rows, rows] += jnp.where(i0 == i1, jnp.broadcast_to(amount, (128, 128)), 0.0)
    i0 = lax.broadcasted_iota(jnp.int32, (KEYS, KEYS), 0)
    i1 = lax.broadcasted_iota(jnp.int32, (KEYS, KEYS), 1)
    m_ref[...] = jnp.where(i0 == i1, 1.0, 0.0).astype(F32)
    for s in range(nsuper):
        following = None
        for j in range(8):
            following = factor16(R, 128 * s + 16 * j, s, j, nt, following)
        us = R[128 * s : 128 * s + 128, 128 * s + 128 :]
        h, m, l = split3(us)
        right = [jnp.concatenate([h, m], 0), jnp.concatenate([h, l], 0), jnp.concatenate([h, m], 0)]
        for t in range(s + 1, nt):
            c0 = 128 * (t - s - 1)
            lh, lm, ll = split3(jnp.transpose(us[:, c0 : c0 + 128]))
            left = [jnp.concatenate([lh, lh], 1), jnp.concatenate([lm, lh], 1), jnp.concatenate([ll, lm], 1)]
            update = (
                mm(left[0], right[0][:, c0:]) + mm(left[1], right[1][:, c0:]) + mm(left[2], right[2][:, c0:])
            )
            if t < nsuper:
                R[128 * t : 128 * t + 128, 128 * t :] -= update
            else:
                q = 128 * (t - nsuper)
                m_ref[q : q + 128, q:] -= update
    m_ref[128:, :128] = jnp.transpose(m_ref[:128, 128:])


def factor(ridge, kp, sums):
    vmem = pl.BlockSpec(memory_space=pltpu.VMEM)
    return pl.pallas_call(
        factor_kernel,
        out_shape=(
            jax.ShapeDtypeStruct((2 * PANEL, 2 * PANEL + KEYS), F32),
            jax.ShapeDtypeStruct((KEYS, KEYS), F32),
            jax.ShapeDtypeStruct((8, 128), F32),
        ),
        in_specs=[pl.BlockSpec(memory_space=pltpu.SMEM), vmem, vmem],
        out_specs=(vmem, vmem, vmem),
        name="factor",
    )(ridge, kp, sums)


def output_kernel(
    u_ref, m_ref, amount_ref, win_ref, wide_ref, pa_out, pb_out, tr_out, fw_out,
    kt, pa, pb, tr, fw, sems,
):
    row, col = lax.axis_index("row"), lax.axis_index("col")
    z, y = row // YS, lax.rem(row, YS)
    kt[...] = jnp.transpose(win_ref[...].astype(F32)).astype(BF16)
    off = pl.multiple_of(64 * lax.rem(y, 2), 64)
    k_rows = kt[pl.ds(off, ROW_UNITS), :]
    qt = u_ref[:, 2 * PANEL :]
    qh, ql = split2(qt)
    q2 = jnp.concatenate([qh, ql], axis=1)
    both = mm_nt(jnp.concatenate([k_rows, k_rows], axis=1), q2)
    pa[...] = both[:, :PANEL]
    pb[...] = both[:, PANEL:]
    i0 = lax.broadcasted_iota(jnp.int32, (PANEL, PANEL), 0)
    i1 = lax.broadcasted_iota(jnp.int32, (PANEL, PANEL), 1)

    @pl.when(row == 0)
    def _():
        pa[:PANEL, :] = jnp.where(i0 >= i1, jnp.transpose(u_ref[:PANEL, :PANEL]), 0.0)
        pb[:PANEL, :] = jnp.zeros((PANEL, PANEL), F32)

    @pl.when(row == YS)
    def _():
        pb[:PANEL, :] = jnp.where(i0 >= i1, jnp.transpose(u_ref[PANEL : 2 * PANEL, PANEL : 2 * PANEL]), 0.0)

    copies = [pltpu.make_async_copy(pa, pa_out, sems.at[0]), pltpu.make_async_copy(pb, pb_out, sems.at[1])]
    for copy in copies:
        copy.start()

    mh, mm_, ml = split3(m_ref[...])
    t = mm(jnp.concatenate([k_rows, k_rows, k_rows], axis=1), jnp.concatenate([mh, mm_, ml], axis=0))
    th, tl = split2(t)
    t2 = jnp.concatenate([th, tl], axis=1)

    v = wide_ref[:, COL_UNITS:]
    v2 = jnp.concatenate([v, v], axis=0)
    fw[...] = mm(t2, v2)

    @pl.when(row == 0)
    def _():
        fw[:PANEL, :] = mm(q2[:PANEL], v2)

    @pl.when(row == YS)
    def _():
        fw[:PANEL, :] = mm(q2[PANEL:], v2)

    copies.append(pltpu.make_async_copy(fw, fw_out, sems.at[2]))
    copies[-1].start()

    for q in range(COL_UNITS // 256):
        lanes = pl.ds(256 * q, 256)
        k = wide_ref[:, 256 * q : 256 * q + 256]
        tr[:, lanes] = mm(t2, jnp.concatenate([k, k], axis=0))

        @pl.when(z == col)
        def _():
            r0 = lax.broadcasted_iota(jnp.int32, (ROW_UNITS, 256), 0)
            r1 = lax.broadcasted_iota(jnp.int32, (ROW_UNITS, 256), 1)
            hit = r1 + (256 * q) == r0 + y * ROW_UNITS
            tr[:, lanes] += jnp.where(hit, amount_ref[0:1, 0:1], 0.0)

        @pl.when((row == 0) | (row == YS))
        def _():
            tr[:PANEL, lanes] = jnp.zeros((PANEL, 256), F32)

        if q == 0:

            @pl.when(col < 2)
            def _():
                tr[:, lanes] = jnp.zeros((ROW_UNITS, 256), F32)

        copies.append(pltpu.make_async_copy(tr.at[:, lanes], tr_out.at[:, lanes], sems.at[3 + q]))
        copies[-1].start()
    for copy in copies:
        copy.wait()


def outputs(u, m, amount, win, wide):
    vmem = pl.BlockSpec(memory_space=pltpu.VMEM)
    anyspace = pl.BlockSpec(memory_space=pl.ANY)
    shapes = [(ROW_UNITS, PANEL), (ROW_UNITS, PANEL), (ROW_UNITS, COL_UNITS), (ROW_UNITS, SHIFTS)]
    return pl.pallas_call(
        output_kernel,
        out_shape=tuple(jax.ShapeDtypeStruct(s, F32) for s in shapes),
        in_specs=[vmem] * 5,
        out_specs=(anyspace,) * 4,
        scratch_shapes=[pltpu.VMEM((WIN, KEYS), BF16)]
        + [pltpu.VMEM(s, F32) for s in shapes]
        + [pltpu.SemaphoreType.DMA((3 + COL_UNITS // 256,))],
        name="outputs",
    )(u, m, amount, win, wide)


def on_device(edit_keys, edit_shifts, ridge_scale):
    crit, sums, wide, window = exchange(edit_keys, edit_shifts)
    kp = crit.reshape(KEYS, 2 * PANEL)
    u, m, amount = factor(ridge_scale, kp, sums.reshape(ROWS * COLS, 128))
    return outputs(u, m, amount, window.reshape(KEYS, WIN), wide.reshape(KEYS, WIDE))


def solution(mesh):
    return jax.shard_map(
        on_device,
        mesh=mesh,
        in_specs=(P("row", "col"), P("row", "col"), P()),
        out_specs=(P("row", None), P("row", None), P("row", "col"), P("row", "col")),
        check_vma=False,
    )
```

```python
import functools

import jax
import jax.numpy as jnp
from jax import lax
from jax.experimental import pallas as pl
from jax.experimental.pallas import tpu as pltpu
from jax.sharding import PartitionSpec as P

F32, BF16 = jnp.float32, jnp.bfloat16
PANEL = 256
ROWS, COLS, YS = 32, 8, 4
ZS = ROWS // YS
SLAB = 8
UNITS = 14336
COL_UNITS = UNITS // COLS
ROW_UNITS = UNITS // ROWS
SHIFTS = 512
WIDE = COL_UNITS + SHIFTS
WIN = 512
KEYS = 256
MESH = pl.DeviceIdType.MESH


def split2(x):
    high = x.astype(BF16)
    return high, (x - high.astype(F32)).astype(BF16)


def split3(x):
    high = x.astype(BF16)
    rest = x - high.astype(F32)
    mid = rest.astype(BF16)
    return high, mid, (rest - mid.astype(F32)).astype(BF16)


def mm(a, b):
    return jnp.dot(a, b, preferred_element_type=F32)


def mm_nt(a, b):
    return lax.dot_general(a, b, (((1,), (1,)), ((), ())), preferred_element_type=F32)


def remote(src, dst, send, recv, row, col):
    return pltpu.make_async_remote_copy(
        src_ref=src, dst_ref=dst, send_sem=send, recv_sem=recv, device_id=(row, col), device_id_type=MESH
    )


def row_bcast(v, k):
    return jnp.broadcast_to(v[k : k + 1, :], (8, v.shape[1]))


def factor16(R, base, s, j, nt, diag_next):
    o = 16 * j
    iota = lax.broadcasted_iota(jnp.int32, (8, 128), 0)
    last = j == 7
    ng = 2 if last else 4
    lanes = slice(128 * s, 128 * s + 128)
    T = list(diag_next) if diag_next is not None else [R[base + 8 * g : base + 8 * g + 8, lanes] for g in range(2)]
    for g in range(2, ng):
        T.append(R[base + 8 * g : base + 8 * g + 8, lanes])
    C = [[None] * 4 for _ in range(16)]
    for k in range(16):
        for g in range(k // 8, ng):
            C[k][g] = jnp.broadcast_to(T[g][:, o + k : o + k + 1], (8, 128))
    Y = {t: [R[base + 8 * g : base + 8 * g + 8, 128 * t : 128 * t + 128] for g in range(2)] for t in range(s + 1, nt)}
    rv = [jnp.zeros((8, 128), F32)] * 2
    for k in range(16):
        gk, kk = k // 8, k % 8
        p = row_bcast(C[k][gk], kk)
        rp = 1.0 / p
        rv[gk] = jnp.where(iota == kk, lax.rsqrt(p), rv[gk])
        M = [None] * 4
        for g in range(gk, ng):
            M[g] = C[k][g] * rp
        for jj in range(k + 1, 16):
            c = row_bcast(C[k][jj // 8], jj % 8)
            for g in range(jj // 8, ng):
                C[jj][g] = C[jj][g] - M[g] * c
        M[gk] = None if kk == 7 else jnp.where(iota > kk, M[gk], 0.0)
        yk = row_bcast(T[gk], kk)
        for g in range(gk, ng):
            if M[g] is not None:
                T[g] = T[g] - M[g] * yk
        for t in range(s + 1, nt):
            yk = row_bcast(Y[t][gk], kk)
            for g in range(gk, 2):
                if M[g] is not None:
                    Y[t][g] = Y[t][g] - M[g] * yk
    U = {s: jnp.concatenate([T[0] * rv[0], T[1] * rv[1]], axis=0)}
    for t in range(s + 1, nt):
        U[t] = jnp.concatenate([Y[t][0] * rv[0], Y[t][1] * rv[1]], axis=0)
    for t in range(s, nt):
        R[base : base + 16, 128 * t : 128 * t + 128] = U[t]
    if last:
        return None
    zero = jnp.zeros((16, 128), BF16)
    parts = {t: split3(U[t]) for t in range(s, nt)}
    h, m, l = parts[s]
    left = jnp.concatenate([h, h, m, h, l, m, zero, zero], axis=0)
    left = jnp.transpose(left.astype(F32)).astype(BF16)[16 * (j + 1) :, :]
    below = 16 * (7 - j)
    for t in range(s, nt):
        h, m, l = parts[t]
        right = jnp.concatenate([h, m, h, l, h, m, zero, zero], axis=0)
        if t == s:
            if below > 16:
                R[base + 32 : base + 16 + below, lanes] -= mm(left[16:], right)
        else:
            R[base + 16 : base + 16 + below, 128 * t : 128 * t + 128] -= mm(left, right)
    return T[2], T[3]


XS = COLS // 2
A_LANES = pl.ds(0, 1152)
B_LANES = pl.ds(1152, 1152)
B_HALVES = (pl.ds(1152, 640), pl.ds(1792, 512))


def fused_kernel(
    ridge, keys, shifts, wide, window, q2_out, m_ref, amount_ref, u_out,
    crit, sums, own_sum, x_sums, R,
    s_local, s_x, r_x, s_r, r_r, s_p, r_p, s_y, r_y, s_a, r_a, s_b, r_b, s_yb, r_yb, s_w, r_w, s_v, r_v,
):
    row, col = lax.axis_index("row"), lax.axis_index("col")
    z, y = row // YS, lax.rem(row, YS)
    x, core = col // 2, lax.rem(col, 2)
    partner = 2 * x + 1 - core

    def await_bytes(ref, sem):
        pltpu.make_async_copy(ref, ref, sem).wait()

    barrier = pltpu.get_barrier_semaphore()

    def greet(r, c):
        pl.semaphore_signal(barrier, inc=1, device_id=(r, c), device_id_type=MESH)

    def greet_row(i, carry):
        greet(lax.rem(row + i, ROWS), col)
        return carry

    for i in range(1, XS):
        greet(row, lax.rem(col + 2 * i, COLS))
    greet(row, partner)
    lax.fori_loop(1, ROWS, greet_row, 0)

    k32 = keys[...].astype(F32)
    sq = k32 * k32
    part = sq[:, 0:128]
    for t in range(1, COL_UNITS // 128):
        part = part + sq[:, 128 * t : 128 * (t + 1)]
    own_sum[0] = jnp.sum(part, axis=0, keepdims=True)

    local = [
        pltpu.make_async_copy(keys, wide.at[row, :, pl.ds(0, COL_UNITS)], s_local.at[0]),
        pltpu.make_async_copy(shifts, wide.at[row, :, pl.ds(COL_UNITS, SHIFTS)], s_local.at[1]),
    ]
    for copy in local:
        copy.start()

    @pl.when(col < 2)
    def _():
        copy = pltpu.make_async_copy(keys.at[:, pl.ds(0, PANEL)], crit.at[core, row], s_local.at[2])
        copy.start()
        copy.wait()

    @pl.when(z == col)
    def _():
        for yy in range(YS):
            start = yy * ROW_UNITS - 64 * (yy % 2)

            @pl.when(y == yy)
            def _():
                copy = pltpu.make_async_copy(keys.at[:, pl.ds(start, WIN)], window.at[row], s_local.at[2])
                copy.start()
                copy.wait()

    for copy in local:
        copy.wait()
    pl.semaphore_wait(barrier, ROWS + XS - 1)

    @pl.when(col < 2)
    def _():
        for i in range(1, XS):
            remote(
                keys.at[:, pl.ds(0, PANEL)], crit.at[core, row], s_x.at[0], r_x.at[0], row, lax.rem(col + 2 * i, COLS)
            ).start()

    for i in range(1, XS):
        remote(own_sum.at[0], x_sums.at[x], s_x.at[1], r_x.at[1], row, lax.rem(col + 2 * i, COLS)).start()
    x_sums[x] = own_sum[0]

    @pl.when(col >= 2)
    def _():
        await_bytes(crit.at[0, 0], r_x.at[0])

    def send_slab(i, carry):
        remote(crit.at[core, row], crit.at[core, row], s_r.at[0], r_r.at[0], lax.rem(row + i, ROWS), col).start()
        return carry

    def send_sum(i, carry):
        remote(sums.at[core, row], sums.at[core, row], s_r.at[1], r_r.at[1], lax.rem(row + i, ROWS), col).start()
        return carry

    await_bytes(x_sums.at[pl.ds(0, XS - 1)], r_x.at[1])
    sums[core, row] = jnp.sum(x_sums[...], axis=0)
    lax.fori_loop(1, ROWS, send_slab, 0)
    lax.fori_loop(1, ROWS, send_sum, 0)
    await_bytes(crit.at[0, pl.ds(0, ROWS - 1)], r_r.at[0])
    await_bytes(sums.at[0, pl.ds(0, ROWS - 1)], r_r.at[1])

    remote(crit.at[core], crit.at[core], s_p.at[0], r_p.at[0], row, partner).start()
    remote(sums.at[core], sums.at[core], s_p.at[1], r_p.at[1], row, partner).start()

    up = lax.rem(z + 1, ZS) * YS
    down = lax.rem(z + ZS - 1, ZS) * YS

    def over_y(slot, lanes, send, recv):
        for i in range(1, YS):
            ref = wide.at[slot * YS + y, :, lanes]
            remote(ref, ref, send, recv, z * YS + lax.rem(y + i, YS), col).start()

    def round_b(step):
        for way, (source, target) in enumerate(((lax.rem(z + ZS - step, ZS), up), (lax.rem(z + step, ZS), down))):
            lanes = B_LANES if step < 3 else B_HALVES[way]
            ref = wide.at[source * YS + y, :, lanes]
            remote(ref, ref, s_b.at[way, step], r_b.at[way, step], target + y, col).start()

    def wait_b(step, sems):
        for way in range(2):
            lanes = B_LANES if step < 3 else B_HALVES[way]
            await_bytes(wide.at[0, :, lanes], sems.at[way, step])

    def pairs_a(step, way):
        return (0, 1) if step < 3 else (way,)

    def round_a(step):
        for pair in range(2):
            for way, (source, target) in enumerate(((lax.rem(z + ZS - step, ZS), up), (lax.rem(z + step, ZS), down))):
                if step > 0:
                    await_bytes(wide.at[pl.ds(0, 2), :, A_LANES], r_a.at[way, step - 1, pair])
                if pair in pairs_a(step, way):
                    ref = wide.at[pl.ds(source * YS + 2 * pair, 2), :, A_LANES]
                    remote(ref, ref, s_a.at[way, step, pair], r_a.at[way, step, pair], target + y, col).start()

    def b_over_y(step):
        if step < 3:
            over_y(lax.rem(z + ZS - step - 1, ZS), B_LANES, s_yb.at[0, step], r_yb.at[0, step])
            over_y(lax.rem(z + step + 1, ZS), B_LANES, s_yb.at[1, step], r_yb.at[1, step])
        else:
            over_y(lax.rem(z + ZS // 2, ZS), B_LANES, s_yb.at[0, step], r_yb.at[0, step])

    over_y(z, pl.ds(0, WIDE), s_y, r_y)
    round_b(0)

    for yy in range(YS):
        start = yy * ROW_UNITS - 64 * (yy % 2)
        target = col * YS + yy
        for i in range(XS):

            @pl.when((target != row) | (i != x))
            def _():
                remote(keys.at[:, pl.ds(start, WIN)], window.at[row], s_w, r_w, target, 2 * i + core).start()

    def swap_window():
        @pl.when(core == lax.rem(z, 2))
        def _():
            @pl.when(col == z)
            def _():
                await_bytes(window.at[pl.ds(0, ROWS - 1)], r_w)

            @pl.when(col != z)
            def _():
                await_bytes(window, r_w)

            remote(window, window, s_v, r_v, row, partner).start()

    def hook1():
        await_bytes(wide.at[pl.ds(0, YS - 1)], r_y)
        round_a(0)
        wait_b(0, r_b)
        round_b(1)
        b_over_y(0)

    def hook2():
        round_a(1)
        wait_b(1, r_b)
        round_b(2)
        b_over_y(1)

    def hook3():
        round_a(2)
        wait_b(2, r_b)
        round_b(3)
        b_over_y(2)

    def hook4():
        round_a(3)
        wait_b(3, r_b)
        b_over_y(3)

    hooks = {3: hook1, 9: hook2, 15: hook3, 21: hook4, 24: swap_window}

    await_bytes(crit.at[0], r_p.at[0])
    await_bytes(sums.at[0], r_p.at[1])

    nsuper = 4
    n = 2 * PANEL
    nt = nsuper + 2
    total = jnp.sum(sums[0] + sums[1], axis=0)
    total = jnp.sum(total, axis=1, keepdims=True)
    amount = ridge[0] * total / UNITS
    amount_ref[...] = jnp.broadcast_to(amount, (8, 128))
    first = crit[0].astype(F32).reshape(KEYS, PANEL)
    second = crit[1].astype(F32).reshape(KEYS, PANEL)
    kp32 = jnp.concatenate([first, second], axis=1)
    kp = kp32.astype(BF16)
    kpt = jnp.transpose(kp32)
    R[:, n:] = kpt
    kptb = kpt.astype(BF16)
    i0 = lax.broadcasted_iota(jnp.int32, (128, 128), 0)
    i1 = lax.broadcasted_iota(jnp.int32, (128, 128), 1)
    for s in range(nsuper):
        rows = slice(128 * s, 128 * s + 128)
        R[rows, 128 * s : n] = mm(kptb[rows, :], kp[:, 128 * s :])
        R[rows, rows] += jnp.where(i0 == i1, jnp.broadcast_to(amount, (128, 128)), 0.0)
    i0 = lax.broadcasted_iota(jnp.int32, (KEYS, KEYS), 0)
    i1 = lax.broadcasted_iota(jnp.int32, (KEYS, KEYS), 1)
    m_ref[...] = jnp.where(i0 == i1, 1.0, 0.0).astype(F32)
    for s in range(nsuper):
        following = None
        for j in range(8):
            following = factor16(R, 128 * s + 16 * j, s, j, nt, following)
            if 8 * s + j in hooks:
                hooks[8 * s + j]()
        us = R[128 * s : 128 * s + 128, 128 * s + 128 :]
        h, m, l = split3(us)
        right = [jnp.concatenate([h, m], 0), jnp.concatenate([h, l], 0), jnp.concatenate([h, m], 0)]
        for t in range(s + 1, nt):
            c0 = 128 * (t - s - 1)
            lh, lm, ll = split3(jnp.transpose(us[:, c0 : c0 + 128]))
            left = [jnp.concatenate([lh, lh], 1), jnp.concatenate([lm, lh], 1), jnp.concatenate([ll, lm], 1)]
            update = (
                mm(left[0], right[0][:, c0:]) + mm(left[1], right[1][:, c0:]) + mm(left[2], right[2][:, c0:])
            )
            if t < nsuper:
                R[128 * t : 128 * t + 128, 128 * t :] -= update
            else:
                q = 128 * (t - nsuper)
                m_ref[q : q + 128, q:] -= update
    m_ref[128:, :128] = jnp.transpose(m_ref[:128, 128:])
    qh, ql = split2(R[:, n:])
    q2_out[...] = jnp.concatenate([qh, ql], axis=1)

    for half in range(2):

        @pl.when(row == YS * half)
        def _():
            part = pl.ds(PANEL * half, PANEL)
            copy = pltpu.make_async_copy(R.at[part, part], u_out, s_local.at[2])
            copy.start()
            copy.wait()

    for way in range(2):
        for pair in pairs_a(3, way):
            await_bytes(wide.at[pl.ds(0, 2), :, A_LANES], r_a.at[way, 3, pair])
    for step in range(4):
        for way in range(2 if step < 3 else 1):
            await_bytes(wide.at[pl.ds(0, YS - 1), :, B_LANES], r_yb.at[way, step])

    @pl.when(core != lax.rem(z, 2))
    def _():
        await_bytes(window, r_v)

    @pl.when(col < 2)
    def _():
        await_bytes(crit.at[0, pl.ds(0, XS - 1)], s_x.at[0])

    await_bytes(x_sums.at[pl.ds(0, XS - 1)], s_x.at[1])
    await_bytes(crit.at[0, pl.ds(0, ROWS - 1)], s_r.at[0])
    await_bytes(sums.at[0, pl.ds(0, ROWS - 1)], s_r.at[1])
    await_bytes(crit.at[0], s_p.at[0])
    await_bytes(sums.at[0], s_p.at[1])
    await_bytes(wide.at[pl.ds(0, YS - 1)], s_y)
    for step in range(4):
        wait_b(step, s_b)
        for way in range(2):
            for pair in pairs_a(step, way):
                await_bytes(wide.at[pl.ds(0, 2), :, A_LANES], s_a.at[way, step, pair])
        for way in range(2 if step < 3 else 1):
            await_bytes(wide.at[pl.ds(0, YS - 1), :, B_LANES], s_yb.at[way, step])

    @pl.when(z == col)
    def _():
        await_bytes(window.at[pl.ds(0, YS * XS - 1)], s_w)

    @pl.when(z != col)
    def _():
        await_bytes(window.at[pl.ds(0, YS * XS)], s_w)

    @pl.when(core == lax.rem(z, 2))
    def _():
        await_bytes(window, s_v)


def fused(ridge, keys, shifts):
    dma = pltpu.SemaphoreType.DMA
    vmem = pl.BlockSpec(memory_space=pltpu.VMEM)
    anyspace = pl.BlockSpec(memory_space=pl.ANY)
    return pl.pallas_call(
        fused_kernel,
        out_shape=(
            jax.ShapeDtypeStruct((ROWS, SLAB, WIDE), BF16),
            jax.ShapeDtypeStruct((ROWS, SLAB, WIN), BF16),
            jax.ShapeDtypeStruct((2 * PANEL, 2 * KEYS), BF16),
            jax.ShapeDtypeStruct((KEYS, KEYS), F32),
            jax.ShapeDtypeStruct((8, 128), F32),
            jax.ShapeDtypeStruct((PANEL, PANEL), F32),
        ),
        in_specs=[pl.BlockSpec(memory_space=pltpu.SMEM), vmem, vmem],
        out_specs=(anyspace, anyspace, vmem, vmem, vmem, anyspace),
        scratch_shapes=[
            pltpu.VMEM((2, ROWS, SLAB, PANEL), BF16),
            pltpu.VMEM((2, ROWS, 1, 128), F32),
            pltpu.VMEM((1, 1, 128), F32),
            pltpu.VMEM((XS, 1, 128), F32),
            pltpu.VMEM((2 * PANEL, 2 * PANEL + KEYS), F32),
            dma((3,)), dma((2,)), dma((2,)), dma((2,)), dma((2,)), dma((2,)), dma((2,)), dma, dma,
            dma((2, 4, 2)), dma((2, 4, 2)), dma((2, 4)), dma((2, 4)), dma((2, 4)), dma((2, 4)),
            dma, dma, dma, dma,
        ],
        compiler_params=pltpu.CompilerParams(collective_id=0, has_side_effects=True),
        name="fused",
    )(ridge, keys, shifts)


def output_kernel(
    q2_ref, m_ref, amount_ref, u_ref, win_ref, wide_ref, pa_out, pb_out, tr_out, fw_out,
    kt, pa, pb, tr, fw, sems,
):
    row, col = lax.axis_index("row"), lax.axis_index("col")
    z, y = row // YS, lax.rem(row, YS)
    kt[...] = jnp.transpose(win_ref[...].astype(F32)).astype(BF16)
    off = pl.multiple_of(64 * lax.rem(y, 2), 64)
    k_rows = kt[pl.ds(off, ROW_UNITS), :]
    q2 = q2_ref[...]
    both = mm_nt(jnp.concatenate([k_rows, k_rows], axis=1), q2)
    pa[...] = both[:, :PANEL]
    pb[...] = both[:, PANEL:]
    i0 = lax.broadcasted_iota(jnp.int32, (PANEL, PANEL), 0)
    i1 = lax.broadcasted_iota(jnp.int32, (PANEL, PANEL), 1)

    @pl.when(row == 0)
    def _():
        pa[:PANEL, :] = jnp.where(i0 >= i1, jnp.transpose(u_ref[...]), 0.0)
        pb[:PANEL, :] = jnp.zeros((PANEL, PANEL), F32)

    @pl.when(row == YS)
    def _():
        pb[:PANEL, :] = jnp.where(i0 >= i1, jnp.transpose(u_ref[...]), 0.0)

    copies = [pltpu.make_async_copy(pa, pa_out, sems.at[0]), pltpu.make_async_copy(pb, pb_out, sems.at[1])]
    for copy in copies:
        copy.start()

    mh, mm_, ml = split3(m_ref[...])
    t = mm(jnp.concatenate([k_rows, k_rows, k_rows], axis=1), jnp.concatenate([mh, mm_, ml], axis=0))
    th, tl = split2(t)
    t2 = jnp.concatenate([th, tl], axis=1)

    v = wide_ref[:, COL_UNITS:]
    v2 = jnp.concatenate([v, v], axis=0)
    fw[...] = mm(t2, v2)

    @pl.when(row == 0)
    def _():
        fw[:PANEL, :] = mm(q2[:PANEL], v2)

    @pl.when(row == YS)
    def _():
        fw[:PANEL, :] = mm(q2[PANEL:], v2)

    copies.append(pltpu.make_async_copy(fw, fw_out, sems.at[2]))
    copies[-1].start()

    for q in range(COL_UNITS // 256):
        lanes = pl.ds(256 * q, 256)
        k = wide_ref[:, 256 * q : 256 * q + 256]
        tr[:, lanes] = mm(t2, jnp.concatenate([k, k], axis=0))

        @pl.when(z == col)
        def _():
            r0 = lax.broadcasted_iota(jnp.int32, (ROW_UNITS, 256), 0)
            r1 = lax.broadcasted_iota(jnp.int32, (ROW_UNITS, 256), 1)
            hit = r1 + (256 * q) == r0 + y * ROW_UNITS
            tr[:, lanes] += jnp.where(hit, amount_ref[0:1, 0:1], 0.0)

        @pl.when((row == 0) | (row == YS))
        def _():
            tr[:PANEL, lanes] = jnp.zeros((PANEL, 256), F32)

        if q == 0:

            @pl.when(col < 2)
            def _():
                tr[:, lanes] = jnp.zeros((ROW_UNITS, 256), F32)

        copies.append(pltpu.make_async_copy(tr.at[:, lanes], tr_out.at[:, lanes], sems.at[3 + q]))
        copies[-1].start()
    for copy in copies:
        copy.wait()


def outputs(q2, m, amount, u, win, wide):
    vmem = pl.BlockSpec(memory_space=pltpu.VMEM)
    anyspace = pl.BlockSpec(memory_space=pl.ANY)
    shapes = [(ROW_UNITS, PANEL), (ROW_UNITS, PANEL), (ROW_UNITS, COL_UNITS), (ROW_UNITS, SHIFTS)]
    return pl.pallas_call(
        output_kernel,
        out_shape=tuple(jax.ShapeDtypeStruct(s, F32) for s in shapes),
        in_specs=[vmem] * 6,
        out_specs=(anyspace,) * 4,
        scratch_shapes=[pltpu.VMEM((WIN, KEYS), BF16)]
        + [pltpu.VMEM(s, F32) for s in shapes]
        + [pltpu.SemaphoreType.DMA((3 + COL_UNITS // 256,))],
        name="outputs",
    )(q2, m, amount, u, win, wide)


def on_device(edit_keys, edit_shifts, ridge_scale):
    wide, window, q2, m, amount, u = fused(ridge_scale, edit_keys, edit_shifts)
    return outputs(q2, m, amount, u, window.reshape(KEYS, WIN), wide.reshape(KEYS, WIDE))


def solution(mesh):
    return jax.shard_map(
        on_device,
        mesh=mesh,
        in_specs=(P("row", "col"), P("row", "col"), P()),
        out_specs=(P("row", None), P("row", None), P("row", "col"), P("row", "col")),
        check_vma=False,
    )
```

```python
import functools

import jax
import jax.numpy as jnp
from jax import lax
from jax.experimental import pallas as pl
from jax.experimental.pallas import tpu as pltpu
from jax.sharding import PartitionSpec as P

F32, BF16 = jnp.float32, jnp.bfloat16
PANEL = 256
ROWS, COLS, YS = 32, 8, 4
ZS = ROWS // YS
SLAB = 8
UNITS = 14336
COL_UNITS = UNITS // COLS
ROW_UNITS = UNITS // ROWS
SHIFTS = 512
WIDE = COL_UNITS + SHIFTS
WIN = 512
KEYS = 256
MESH = pl.DeviceIdType.MESH


def split2(x):
    high = x.astype(BF16)
    return high, (x - high.astype(F32)).astype(BF16)


def split3(x):
    high = x.astype(BF16)
    rest = x - high.astype(F32)
    mid = rest.astype(BF16)
    return high, mid, (rest - mid.astype(F32)).astype(BF16)


def mm(a, b):
    return jnp.dot(a, b, preferred_element_type=F32)


def mm_nt(a, b):
    return lax.dot_general(a, b, (((1,), (1,)), ((), ())), preferred_element_type=F32)


def remote(src, dst, send, recv, row, col):
    return pltpu.make_async_remote_copy(
        src_ref=src, dst_ref=dst, send_sem=send, recv_sem=recv, device_id=(row, col), device_id_type=MESH
    )


def row_bcast(v, k):
    return jnp.broadcast_to(v[k : k + 1, :], (8, v.shape[1]))


def factor16(R, base, s, j, nt, diag_next):
    o = 16 * j
    iota = lax.broadcasted_iota(jnp.int32, (8, 128), 0)
    last = j == 7
    ng = 2 if last else 4
    lanes = slice(128 * s, 128 * s + 128)
    T = list(diag_next) if diag_next is not None else [R[base + 8 * g : base + 8 * g + 8, lanes] for g in range(2)]
    for g in range(2, ng):
        T.append(R[base + 8 * g : base + 8 * g + 8, lanes])
    C = [[None] * 4 for _ in range(16)]
    for k in range(16):
        for g in range(k // 8, ng):
            C[k][g] = jnp.broadcast_to(T[g][:, o + k : o + k + 1], (8, 128))
    Y = {t: [R[base + 8 * g : base + 8 * g + 8, 128 * t : 128 * t + 128] for g in range(2)] for t in range(s + 1, nt)}
    rv = [jnp.zeros((8, 128), F32)] * 2
    for k in range(16):
        gk, kk = k // 8, k % 8
        p = row_bcast(C[k][gk], kk)
        rp = 1.0 / p
        rv[gk] = jnp.where(iota == kk, lax.rsqrt(p), rv[gk])
        M = [None] * 4
        for g in range(gk, ng):
            M[g] = C[k][g] * rp
        for jj in range(k + 1, 16):
            c = row_bcast(C[k][jj // 8], jj % 8)
            for g in range(jj // 8, ng):
                C[jj][g] = C[jj][g] - M[g] * c
        M[gk] = None if kk == 7 else jnp.where(iota > kk, M[gk], 0.0)
        yk = row_bcast(T[gk], kk)
        for g in range(gk, ng):
            if M[g] is not None:
                T[g] = T[g] - M[g] * yk
        for t in range(s + 1, nt):
            yk = row_bcast(Y[t][gk], kk)
            for g in range(gk, 2):
                if M[g] is not None:
                    Y[t][g] = Y[t][g] - M[g] * yk
    U = {s: jnp.concatenate([T[0] * rv[0], T[1] * rv[1]], axis=0)}
    for t in range(s + 1, nt):
        U[t] = jnp.concatenate([Y[t][0] * rv[0], Y[t][1] * rv[1]], axis=0)
    for t in range(s, nt):
        R[base : base + 16, 128 * t : 128 * t + 128] = U[t]
    if last:
        return None
    zero = jnp.zeros((16, 128), BF16)
    parts = {t: split3(U[t]) for t in range(s, nt)}
    h, m, l = parts[s]
    left = jnp.concatenate([h, h, m, h, l, m, zero, zero], axis=0)
    left = jnp.transpose(left.astype(F32)).astype(BF16)[16 * (j + 1) :, :]
    below = 16 * (7 - j)
    for t in range(s, nt):
        h, m, l = parts[t]
        right = jnp.concatenate([h, m, h, l, h, m, zero, zero], axis=0)
        if t == s:
            if below > 16:
                R[base + 32 : base + 16 + below, lanes] -= mm(left[16:], right)
        else:
            R[base + 16 : base + 16 + below, 128 * t : 128 * t + 128] -= mm(left, right)
    return T[2], T[3]


XS = COLS // 2
HALVES = (pl.ds(0, 1152), pl.ds(1152, 1152))


def fused_kernel(
    ridge, keys, shifts, wide, window, q2_out, m_ref, amount_ref, u_out,
    crit, sums, own_sum, x_sums, R,
    s_local, s_x, r_x, s_r, r_r, s_p, r_p, s_own, r_own, s_z, r_z, s_y, r_y, s_w, r_w, s_v, r_v,
):
    row, col = lax.axis_index("row"), lax.axis_index("col")
    z, y = row // YS, lax.rem(row, YS)
    x, core = col // 2, lax.rem(col, 2)
    partner = 2 * x + 1 - core

    def await_bytes(ref, sem):
        pltpu.make_async_copy(ref, ref, sem).wait()

    barrier = pltpu.get_barrier_semaphore()

    def greet(r, c):
        pl.semaphore_signal(barrier, inc=1, device_id=(r, c), device_id_type=MESH)

    def greet_row(i, carry):
        greet(lax.rem(row + i, ROWS), col)
        return carry

    for i in range(1, XS):
        greet(row, lax.rem(col + 2 * i, COLS))
    greet(row, partner)
    lax.fori_loop(1, ROWS, greet_row, 0)

    k32 = keys[...].astype(F32)
    sq = k32 * k32
    part = sq[:, 0:128]
    for t in range(1, COL_UNITS // 128):
        part = part + sq[:, 128 * t : 128 * (t + 1)]
    own_sum[0] = jnp.sum(part, axis=0, keepdims=True)

    local = [
        pltpu.make_async_copy(keys, wide.at[row, :, pl.ds(0, COL_UNITS)], s_local.at[0]),
        pltpu.make_async_copy(shifts, wide.at[row, :, pl.ds(COL_UNITS, SHIFTS)], s_local.at[1]),
    ]
    for copy in local:
        copy.start()

    @pl.when(col < 2)
    def _():
        copy = pltpu.make_async_copy(keys.at[:, pl.ds(0, PANEL)], crit.at[core, row], s_local.at[2])
        copy.start()
        copy.wait()

    @pl.when(z == col)
    def _():
        for yy in range(YS):
            start = yy * ROW_UNITS - 64 * (yy % 2)

            @pl.when(y == yy)
            def _():
                copy = pltpu.make_async_copy(keys.at[:, pl.ds(start, WIN)], window.at[row], s_local.at[2])
                copy.start()
                copy.wait()

    for copy in local:
        copy.wait()
    pl.semaphore_wait(barrier, ROWS + XS - 1)

    up = lax.rem(z + 1, ZS) * YS
    down = lax.rem(z + ZS - 1, ZS) * YS

    def over_y(slot, send, recv):
        for i in range(1, YS):
            ref = wide.at[slot * YS + y]
            remote(ref, ref, send, recv, z * YS + lax.rem(y + i, YS), col).start()

    def step_ref(slot, step, way):
        ref = wide.at[slot * YS + y]
        return ref if step < 3 else ref.at[:, HALVES[way]]

    def round_z(step):
        for way, (source, target) in enumerate(((lax.rem(z + ZS - step, ZS), up), (lax.rem(z + step, ZS), down))):
            ref = step_ref(source, step, way)
            remote(ref, ref, s_z.at[way, step], r_z.at[way, step], target + y, col).start()

    def wait_z(step, sems):
        for way in range(2):
            await_bytes(step_ref(0, step, way), sems.at[way, step])

    def spread_y(step):
        over_y(lax.rem(z + ZS - step - 1, ZS), s_y.at[0, step], r_y.at[0, step])
        if step < 3:
            over_y(lax.rem(z + step + 1, ZS), s_y.at[1, step], r_y.at[1, step])

    @pl.when(col < 2)
    def _():
        for i in range(1, XS):
            remote(
                keys.at[:, pl.ds(0, PANEL)], crit.at[core, row], s_x.at[0], r_x.at[0], row, lax.rem(col + 2 * i, COLS)
            ).start()

    for i in range(1, XS):
        remote(own_sum.at[0], x_sums.at[x], s_x.at[1], r_x.at[1], row, lax.rem(col + 2 * i, COLS)).start()
    x_sums[x] = own_sum[0]
    over_y(z, s_own, r_own)
    round_z(0)

    @pl.when(col >= 2)
    def _():
        await_bytes(crit.at[0, 0], r_x.at[0])

    def send_slab(i, carry):
        remote(crit.at[core, row], crit.at[core, row], s_r.at[0], r_r.at[0], lax.rem(row + i, ROWS), col).start()
        return carry

    def send_sum(i, carry):
        remote(sums.at[core, row], sums.at[core, row], s_r.at[1], r_r.at[1], lax.rem(row + i, ROWS), col).start()
        return carry

    await_bytes(x_sums.at[pl.ds(0, XS - 1)], r_x.at[1])
    sums[core, row] = jnp.sum(x_sums[...], axis=0)
    lax.fori_loop(1, ROWS, send_slab, 0)
    lax.fori_loop(1, ROWS, send_sum, 0)
    wait_z(0, r_z)
    round_z(1)
    await_bytes(crit.at[0, pl.ds(0, ROWS - 1)], r_r.at[0])
    await_bytes(sums.at[0, pl.ds(0, ROWS - 1)], r_r.at[1])

    remote(crit.at[core], crit.at[core], s_p.at[0], r_p.at[0], row, partner).start()
    remote(sums.at[core], sums.at[core], s_p.at[1], r_p.at[1], row, partner).start()

    spread_y(0)
    wait_z(1, r_z)
    round_z(2)
    spread_y(1)

    for yy in range(YS):
        start = yy * ROW_UNITS - 64 * (yy % 2)
        target = col * YS + yy
        for i in range(XS):

            @pl.when((target != row) | (i != x))
            def _():
                remote(keys.at[:, pl.ds(start, WIN)], window.at[row], s_w, r_w, target, 2 * i + core).start()

    def swap_window():
        @pl.when(core == lax.rem(z, 2))
        def _():
            @pl.when(col == z)
            def _():
                await_bytes(window.at[pl.ds(0, ROWS - 1)], r_w)

            @pl.when(col != z)
            def _():
                await_bytes(window, r_w)

            remote(window, window, s_v, r_v, row, partner).start()

    def hook_three():
        wait_z(2, r_z)
        round_z(3)
        spread_y(2)

    def hook_four():
        wait_z(3, r_z)
        spread_y(3)

    hooks = {4: hook_three, 12: hook_four, 24: swap_window}

    await_bytes(crit.at[0], r_p.at[0])
    await_bytes(sums.at[0], r_p.at[1])

    nsuper = 4
    n = 2 * PANEL
    nt = nsuper + 2
    total = jnp.sum(sums[0] + sums[1], axis=0)
    total = jnp.sum(total, axis=1, keepdims=True)
    amount = ridge[0] * total / UNITS
    amount_ref[...] = jnp.broadcast_to(amount, (8, 128))
    first = crit[0].astype(F32).reshape(KEYS, PANEL)
    second = crit[1].astype(F32).reshape(KEYS, PANEL)
    kp32 = jnp.concatenate([first, second], axis=1)
    kp = kp32.astype(BF16)
    kpt = jnp.transpose(kp32)
    R[:, n:] = kpt
    kptb = kpt.astype(BF16)
    i0 = lax.broadcasted_iota(jnp.int32, (128, 128), 0)
    i1 = lax.broadcasted_iota(jnp.int32, (128, 128), 1)
    for s in range(nsuper):
        rows = slice(128 * s, 128 * s + 128)
        R[rows, 128 * s : n] = mm(kptb[rows, :], kp[:, 128 * s :])
        R[rows, rows] += jnp.where(i0 == i1, jnp.broadcast_to(amount, (128, 128)), 0.0)
    i0 = lax.broadcasted_iota(jnp.int32, (KEYS, KEYS), 0)
    i1 = lax.broadcasted_iota(jnp.int32, (KEYS, KEYS), 1)
    m_ref[...] = jnp.where(i0 == i1, 1.0, 0.0).astype(F32)
    for s in range(nsuper):
        following = None
        for j in range(8):
            following = factor16(R, 128 * s + 16 * j, s, j, nt, following)
            if 8 * s + j in hooks:
                hooks[8 * s + j]()
        us = R[128 * s : 128 * s + 128, 128 * s + 128 :]
        h, m, l = split3(us)
        right = [jnp.concatenate([h, m], 0), jnp.concatenate([h, l], 0), jnp.concatenate([h, m], 0)]
        for t in range(s + 1, nt):
            c0 = 128 * (t - s - 1)
            lh, lm, ll = split3(jnp.transpose(us[:, c0 : c0 + 128]))
            left = [jnp.concatenate([lh, lh], 1), jnp.concatenate([lm, lh], 1), jnp.concatenate([ll, lm], 1)]
            update = (
                mm(left[0], right[0][:, c0:]) + mm(left[1], right[1][:, c0:]) + mm(left[2], right[2][:, c0:])
            )
            if t < nsuper:
                R[128 * t : 128 * t + 128, 128 * t :] -= update
            else:
                q = 128 * (t - nsuper)
                m_ref[q : q + 128, q:] -= update
    m_ref[128:, :128] = jnp.transpose(m_ref[:128, 128:])
    qh, ql = split2(R[:, n:])
    q2_out[...] = jnp.concatenate([qh, ql], axis=1)

    for half in range(2):

        @pl.when(row == YS * half)
        def _():
            part = pl.ds(PANEL * half, PANEL)
            copy = pltpu.make_async_copy(R.at[part, part], u_out, s_local.at[2])
            copy.start()
            copy.wait()

    await_bytes(wide.at[pl.ds(0, YS - 1)], r_own)
    for step in range(4):
        for way in range(2 if step < 3 else 1):
            await_bytes(wide.at[pl.ds(0, YS - 1)], r_y.at[way, step])

    @pl.when(core != lax.rem(z, 2))
    def _():
        await_bytes(window, r_v)

    @pl.when(col < 2)
    def _():
        await_bytes(crit.at[0, pl.ds(0, XS - 1)], s_x.at[0])

    await_bytes(x_sums.at[pl.ds(0, XS - 1)], s_x.at[1])
    await_bytes(crit.at[0, pl.ds(0, ROWS - 1)], s_r.at[0])
    await_bytes(sums.at[0, pl.ds(0, ROWS - 1)], s_r.at[1])
    await_bytes(crit.at[0], s_p.at[0])
    await_bytes(sums.at[0], s_p.at[1])
    await_bytes(wide.at[pl.ds(0, YS - 1)], s_own)
    for step in range(4):
        wait_z(step, s_z)
        for way in range(2 if step < 3 else 1):
            await_bytes(wide.at[pl.ds(0, YS - 1)], s_y.at[way, step])

    @pl.when(z == col)
    def _():
        await_bytes(window.at[pl.ds(0, YS * XS - 1)], s_w)

    @pl.when(z != col)
    def _():
        await_bytes(window.at[pl.ds(0, YS * XS)], s_w)

    @pl.when(core == lax.rem(z, 2))
    def _():
        await_bytes(window, s_v)


def fused(ridge, keys, shifts):
    dma = pltpu.SemaphoreType.DMA
    vmem = pl.BlockSpec(memory_space=pltpu.VMEM)
    anyspace = pl.BlockSpec(memory_space=pl.ANY)
    return pl.pallas_call(
        fused_kernel,
        out_shape=(
            jax.ShapeDtypeStruct((ROWS, SLAB, WIDE), BF16),
            jax.ShapeDtypeStruct((ROWS, SLAB, WIN), BF16),
            jax.ShapeDtypeStruct((2 * PANEL, 2 * KEYS), BF16),
            jax.ShapeDtypeStruct((KEYS, KEYS), F32),
            jax.ShapeDtypeStruct((8, 128), F32),
            jax.ShapeDtypeStruct((PANEL, PANEL), F32),
        ),
        in_specs=[pl.BlockSpec(memory_space=pltpu.SMEM), vmem, vmem],
        out_specs=(anyspace, anyspace, vmem, vmem, vmem, anyspace),
        scratch_shapes=[
            pltpu.VMEM((2, ROWS, SLAB, PANEL), BF16),
            pltpu.VMEM((2, ROWS, 1, 128), F32),
            pltpu.VMEM((1, 1, 128), F32),
            pltpu.VMEM((XS, 1, 128), F32),
            pltpu.VMEM((2 * PANEL, 2 * PANEL + KEYS), F32),
            dma((3,)), dma((2,)), dma((2,)), dma((2,)), dma((2,)), dma((2,)), dma((2,)), dma, dma,
            dma((2, 4)), dma((2, 4)), dma((2, 4)), dma((2, 4)),
            dma, dma, dma, dma,
        ],
        compiler_params=pltpu.CompilerParams(collective_id=0, has_side_effects=True),
        name="fused",
    )(ridge, keys, shifts)


def output_kernel(
    q2, m, amount_ref, u_hbm, win, wide, pa_out, pb_out, tr_out, fw_out,
    u, kt, pa, pb, tr, fw, in_sem, sems,
):
    row, col = lax.axis_index("row"), lax.axis_index("col")
    z, y = row // YS, lax.rem(row, YS)
    chunks = COL_UNITS // 256
    special = (row == 0) | (row == YS)

    load_u = pltpu.make_async_copy(u_hbm, u, in_sem)

    @pl.when(special)
    def _():
        load_u.start()

    kt[...] = jnp.transpose(win[...].astype(F32)).astype(BF16)
    off = pl.multiple_of(64 * lax.rem(y, 2), 64)
    k_rows = kt[pl.ds(off, ROW_UNITS), :]
    k_rows2 = jnp.concatenate([k_rows, k_rows], axis=1)
    mh, ml = split2(m[...])
    th, tl = split2(mm(k_rows2, jnp.concatenate([mh, ml], axis=0)))
    t2 = jnp.concatenate([th, tl], axis=1)

    copies = []

    def send(src, dst, sem):
        copies.append(pltpu.make_async_copy(src, dst, sems.at[sem]))
        copies[-1].start()

    def trailing_chunk(q):
        lanes = pl.ds(256 * q, 256)
        k = wide[:, 256 * q : 256 * q + 256]
        tr[:, lanes] = mm(t2, jnp.concatenate([k, k], axis=0))

        @pl.when((z == col) & (y * ROW_UNITS < 256 * (q + 1)) & ((y + 1) * ROW_UNITS > 256 * q))
        def _():
            r0 = lax.broadcasted_iota(jnp.int32, (ROW_UNITS, 256), 0)
            r1 = lax.broadcasted_iota(jnp.int32, (ROW_UNITS, 256), 1)
            hit = r1 + (256 * q) == r0 + y * ROW_UNITS
            tr[:, lanes] += jnp.where(hit, amount_ref[0:1, 0:1], 0.0)

        @pl.when(special)
        def _():
            tr[:PANEL, lanes] = jnp.zeros((PANEL, 256), F32)

        if q == 0:

            @pl.when(col < 2)
            def _():
                tr[:, lanes] = jnp.zeros((ROW_UNITS, 256), F32)

        send(tr.at[:, lanes], tr_out.at[:, lanes], 3 + q)

    for q in range(3):
        trailing_chunk(q)

    both = mm_nt(k_rows2, q2[...])
    pa[...] = both[:, :PANEL]
    pb[...] = both[:, PANEL:]

    @pl.when(special)
    def _():
        load_u.wait()
        i0 = lax.broadcasted_iota(jnp.int32, (PANEL, PANEL), 0)
        i1 = lax.broadcasted_iota(jnp.int32, (PANEL, PANEL), 1)
        lower = jnp.where(i0 >= i1, jnp.transpose(u[...]), 0.0)
        pb[:PANEL, :] = lower

        @pl.when(row == 0)
        def _():
            pa[:PANEL, :] = lower
            pb[:PANEL, :] = jnp.zeros((PANEL, PANEL), F32)

    send(pa, pa_out, 0)
    send(pb, pb_out, 1)

    v = wide[:, COL_UNITS:]
    v2 = jnp.concatenate([v, v], axis=0)
    fw[...] = mm(t2, v2)

    @pl.when(special)
    def _():
        start = pl.multiple_of(PANEL * (row // YS), PANEL)
        fw[:PANEL, :] = mm(q2[pl.ds(start, PANEL), :], v2)

    send(fw, fw_out, 2)
    for q in range(3, chunks):
        trailing_chunk(q)
    for copy in copies:
        copy.wait()


def outputs(q2, m, amount, u, win, wide):
    vmem = pl.BlockSpec(memory_space=pltpu.VMEM)
    anyspace = pl.BlockSpec(memory_space=pl.ANY)
    shapes = [(ROW_UNITS, PANEL), (ROW_UNITS, PANEL), (ROW_UNITS, COL_UNITS), (ROW_UNITS, SHIFTS)]
    chunks = COL_UNITS // 256
    return pl.pallas_call(
        output_kernel,
        out_shape=tuple(jax.ShapeDtypeStruct(s, F32) for s in shapes),
        in_specs=[vmem, vmem, vmem, anyspace, vmem, vmem],
        out_specs=(anyspace,) * 4,
        scratch_shapes=[
            pltpu.VMEM((PANEL, PANEL), F32),
            pltpu.VMEM((WIN, KEYS), BF16),
        ]
        + [pltpu.VMEM(s, F32) for s in shapes]
        + [pltpu.SemaphoreType.DMA, pltpu.SemaphoreType.DMA((3 + chunks,))],
        name="outputs",
    )(q2, m, amount, u, win, wide)


def on_device(edit_keys, edit_shifts, ridge_scale):
    wide, window, q2, m, amount, u = fused(ridge_scale, edit_keys, edit_shifts)
    return outputs(q2, m, amount, u, window.reshape(KEYS, WIN), wide.reshape(KEYS, WIDE))


def solution(mesh):
    return jax.shard_map(
        on_device,
        mesh=mesh,
        in_specs=(P("row", "col"), P("row", "col"), P()),
        out_specs=(P("row", None), P("row", None), P("row", "col"), P("row", "col")),
        check_vma=False,
    )
```

```python
import functools

import jax
import jax.numpy as jnp
from jax import lax
from jax.experimental import pallas as pl
from jax.experimental.pallas import tpu as pltpu
from jax.sharding import PartitionSpec as P

F32, BF16 = jnp.float32, jnp.bfloat16
PANEL = 256
ROWS, COLS, YS = 32, 8, 4
ZS = ROWS // YS
SLAB = 8
UNITS = 14336
COL_UNITS = UNITS // COLS
ROW_UNITS = UNITS // ROWS
SHIFTS = 512
WIDE = COL_UNITS + SHIFTS
WIN = 512
KEYS = 256
MESH = pl.DeviceIdType.MESH


def split2(x):
    high = x.astype(BF16)
    return high, (x - high.astype(F32)).astype(BF16)


def split3(x):
    high = x.astype(BF16)
    rest = x - high.astype(F32)
    mid = rest.astype(BF16)
    return high, mid, (rest - mid.astype(F32)).astype(BF16)


def mm(a, b):
    return jnp.dot(a, b, preferred_element_type=F32)


def mm_nt(a, b):
    return lax.dot_general(a, b, (((1,), (1,)), ((), ())), preferred_element_type=F32)


def remote(src, dst, send, recv, row, col):
    return pltpu.make_async_remote_copy(
        src_ref=src, dst_ref=dst, send_sem=send, recv_sem=recv, device_id=(row, col), device_id_type=MESH
    )


def row_bcast(v, k):
    return jnp.broadcast_to(v[k : k + 1, :], (8, v.shape[1]))


def factor16(R, base, s, j, nt, diag_next, early):
    o = 16 * j
    iota = lax.broadcasted_iota(jnp.int32, (8, 128), 0)
    last = j == 7
    ng = 2 if last else 4
    lanes = slice(128 * s, 128 * s + 128)
    T = list(diag_next) if diag_next is not None else [R[base + 8 * g : base + 8 * g + 8, lanes] for g in range(2)]
    for g in range(2, ng):
        T.append(R[base + 8 * g : base + 8 * g + 8, lanes])
    C = [[None] * 4 for _ in range(16)]
    for k in range(16):
        for g in range(k // 8, ng):
            if early is not None and g == 0:
                C[k][g] = early[k]
            else:
                C[k][g] = jnp.broadcast_to(T[g][:, o + k : o + k + 1], (8, 128))
    ahead = None
    Y = {t: [R[base + 8 * g : base + 8 * g + 8, 128 * t : 128 * t + 128] for g in range(2)] for t in range(s + 1, nt)}
    rv = [jnp.zeros((8, 128), F32)] * 2
    for k in range(16):
        gk, kk = k // 8, k % 8
        p = row_bcast(C[k][gk], kk)
        rp = 1.0 / p
        rv[gk] = jnp.where(iota == kk, lax.rsqrt(p), rv[gk])
        M = [None] * 4
        for g in range(gk, ng):
            M[g] = C[k][g] * rp
        for jj in range(k + 1, 16):
            c = row_bcast(C[k][jj // 8], jj % 8)
            for g in range(jj // 8, ng):
                C[jj][g] = C[jj][g] - M[g] * c
        M[gk] = None if kk == 7 else jnp.where(iota > kk, M[gk], 0.0)
        yk = row_bcast(T[gk], kk)
        for g in range(gk, ng):
            if M[g] is not None:
                T[g] = T[g] - M[g] * yk
        for t in range(s + 1, nt):
            yk = row_bcast(Y[t][gk], kk)
            for g in range(gk, 2):
                if M[g] is not None:
                    Y[t][g] = Y[t][g] - M[g] * yk
        if not last:
            if k == 11:
                ahead = [jnp.broadcast_to(T[2][:, o + 16 + q : o + 17 + q], (8, 128)) for q in range(8)]
            elif k > 11:
                ahead = [ahead[q] - M[2] * row_bcast(C[k][2], q) for q in range(8)]
    U = {s: jnp.concatenate([T[0] * rv[0], T[1] * rv[1]], axis=0)}
    for t in range(s + 1, nt):
        U[t] = jnp.concatenate([Y[t][0] * rv[0], Y[t][1] * rv[1]], axis=0)
    for t in range(s, nt):
        R[base : base + 16, 128 * t : 128 * t + 128] = U[t]
    if last:
        return None, None
    zero = jnp.zeros((16, 128), BF16)
    parts = {t: split3(U[t]) for t in range(s, nt)}
    h, m, l = parts[s]
    left = jnp.concatenate([h, h, m, h, l, m, zero, zero], axis=0)
    left = jnp.transpose(left.astype(F32)).astype(BF16)[16 * (j + 1) :, :]
    below = 16 * (7 - j)
    for t in range(s, nt):
        h, m, l = parts[t]
        right = jnp.concatenate([h, m, h, l, h, m, zero, zero], axis=0)
        if t == s:
            if below > 16:
                R[base + 32 : base + 16 + below, lanes] -= mm(left[16:], right)
        else:
            R[base + 16 : base + 16 + below, 128 * t : 128 * t + 128] -= mm(left, right)
    return (T[2], T[3]), ahead


XS = COLS // 2
HALVES = (pl.ds(0, 1152), pl.ds(1152, 1152))


def fused_kernel(
    ridge, keys, shifts, wide, window, q2_out, m_ref, amount_ref, u_out,
    crit, sums, own_sum, x_sums, R,
    s_local, s_x, r_x, s_r, r_r, s_p, r_p, s_own, r_own, s_z, r_z, s_y, r_y, s_w, r_w, s_v, r_v,
):
    row, col = lax.axis_index("row"), lax.axis_index("col")
    z, y = row // YS, lax.rem(row, YS)
    x, core = col // 2, lax.rem(col, 2)
    partner = 2 * x + 1 - core

    def await_bytes(ref, sem):
        pltpu.make_async_copy(ref, ref, sem).wait()

    barrier = pltpu.get_barrier_semaphore()

    def greet(r, c):
        pl.semaphore_signal(barrier, inc=1, device_id=(r, c), device_id_type=MESH)

    def greet_row(i, carry):
        greet(lax.rem(row + i, ROWS), col)
        return carry

    for i in range(1, XS):
        greet(row, lax.rem(col + 2 * i, COLS))
    greet(row, partner)
    lax.fori_loop(1, ROWS, greet_row, 0)

    k32 = keys[...].astype(F32)
    sq = k32 * k32
    part = sq[:, 0:128]
    for t in range(1, COL_UNITS // 128):
        part = part + sq[:, 128 * t : 128 * (t + 1)]
    own_sum[0] = jnp.sum(part, axis=0, keepdims=True)

    local = [
        pltpu.make_async_copy(keys, wide.at[row, :, pl.ds(0, COL_UNITS)], s_local.at[0]),
        pltpu.make_async_copy(shifts, wide.at[row, :, pl.ds(COL_UNITS, SHIFTS)], s_local.at[1]),
    ]
    for copy in local:
        copy.start()

    @pl.when(col < 2)
    def _():
        copy = pltpu.make_async_copy(keys.at[:, pl.ds(0, PANEL)], crit.at[core, row], s_local.at[2])
        copy.start()
        copy.wait()

    @pl.when(z == col)
    def _():
        for yy in range(YS):
            start = yy * ROW_UNITS - 64 * (yy % 2)

            @pl.when(y == yy)
            def _():
                copy = pltpu.make_async_copy(keys.at[:, pl.ds(start, WIN)], window.at[row], s_local.at[2])
                copy.start()
                copy.wait()

    for copy in local:
        copy.wait()
    pl.semaphore_wait(barrier, ROWS + XS - 1)

    up = lax.rem(z + 1, ZS) * YS
    down = lax.rem(z + ZS - 1, ZS) * YS

    def over_y(slot, send, recv):
        for i in range(1, YS):
            ref = wide.at[slot * YS + y]
            remote(ref, ref, send, recv, z * YS + lax.rem(y + i, YS), col).start()

    def step_ref(slot, step, way):
        ref = wide.at[slot * YS + y]
        return ref if step < 3 else ref.at[:, HALVES[way]]

    def round_z(step):
        for way, (source, target) in enumerate(((lax.rem(z + ZS - step, ZS), up), (lax.rem(z + step, ZS), down))):
            ref = step_ref(source, step, way)
            remote(ref, ref, s_z.at[way, step], r_z.at[way, step], target + y, col).start()

    def wait_z(step, sems):
        for way in range(2):
            await_bytes(step_ref(0, step, way), sems.at[way, step])

    def spread_y(step):
        over_y(lax.rem(z + ZS - step - 1, ZS), s_y.at[0, step], r_y.at[0, step])
        if step < 3:
            over_y(lax.rem(z + step + 1, ZS), s_y.at[1, step], r_y.at[1, step])

    @pl.when(col < 2)
    def _():
        for i in range(1, XS):
            remote(
                keys.at[:, pl.ds(0, PANEL)], crit.at[core, row], s_x.at[0], r_x.at[0], row, lax.rem(col + 2 * i, COLS)
            ).start()

    for i in range(1, XS):
        remote(own_sum.at[0], x_sums.at[x], s_x.at[1], r_x.at[1], row, lax.rem(col + 2 * i, COLS)).start()
    x_sums[x] = own_sum[0]
    over_y(z, s_own, r_own)
    round_z(0)

    @pl.when(col >= 2)
    def _():
        await_bytes(crit.at[0, 0], r_x.at[0])

    def send_slab(i, carry):
        remote(crit.at[core, row], crit.at[core, row], s_r.at[0], r_r.at[0], lax.rem(row + i, ROWS), col).start()
        return carry

    def send_sum(i, carry):
        remote(sums.at[core, row], sums.at[core, row], s_r.at[1], r_r.at[1], lax.rem(row + i, ROWS), col).start()
        return carry

    await_bytes(x_sums.at[pl.ds(0, XS - 1)], r_x.at[1])
    sums[core, row] = jnp.sum(x_sums[...], axis=0)
    lax.fori_loop(1, ROWS, send_slab, 0)
    lax.fori_loop(1, ROWS, send_sum, 0)
    wait_z(0, r_z)
    round_z(1)
    await_bytes(crit.at[0, pl.ds(0, ROWS - 1)], r_r.at[0])
    await_bytes(sums.at[0, pl.ds(0, ROWS - 1)], r_r.at[1])

    remote(crit.at[core], crit.at[core], s_p.at[0], r_p.at[0], row, partner).start()
    remote(sums.at[core], sums.at[core], s_p.at[1], r_p.at[1], row, partner).start()

    spread_y(0)
    wait_z(1, r_z)
    round_z(2)
    spread_y(1)

    for yy in range(YS):
        start = yy * ROW_UNITS - 64 * (yy % 2)
        target = col * YS + yy
        for i in range(XS):

            @pl.when((target != row) | (i != x))
            def _():
                remote(keys.at[:, pl.ds(start, WIN)], window.at[row], s_w, r_w, target, 2 * i + core).start()

    def swap_window():
        @pl.when(core == lax.rem(z, 2))
        def _():
            @pl.when(col == z)
            def _():
                await_bytes(window.at[pl.ds(0, ROWS - 1)], r_w)

            @pl.when(col != z)
            def _():
                await_bytes(window, r_w)

            remote(window, window, s_v, r_v, row, partner).start()

    def hook_three():
        wait_z(2, r_z)
        round_z(3)
        spread_y(2)

    def hook_four():
        wait_z(3, r_z)
        spread_y(3)

    hooks = {7: hook_three, 15: hook_four, 23: swap_window}

    await_bytes(crit.at[0], r_p.at[0])
    await_bytes(sums.at[0], r_p.at[1])

    nsuper = 4
    n = 2 * PANEL
    nt = nsuper + 2
    total = jnp.sum(sums[0] + sums[1], axis=0)
    total = jnp.sum(total, axis=1, keepdims=True)
    amount = ridge[0] * total / UNITS
    amount_ref[...] = jnp.broadcast_to(amount, (8, 128))
    first = crit[0].astype(F32).reshape(KEYS, PANEL)
    second = crit[1].astype(F32).reshape(KEYS, PANEL)
    kp32 = jnp.concatenate([first, second], axis=1)
    kp = kp32.astype(BF16)
    kpt = jnp.transpose(kp32)
    R[:, n:] = kpt
    kptb = kpt.astype(BF16)
    i0 = lax.broadcasted_iota(jnp.int32, (128, 128), 0)
    i1 = lax.broadcasted_iota(jnp.int32, (128, 128), 1)
    for s in range(nsuper):
        rows = slice(128 * s, 128 * s + 128)
        R[rows, 128 * s : n] = mm(kptb[rows, :], kp[:, 128 * s :])
        R[rows, rows] += jnp.where(i0 == i1, jnp.broadcast_to(amount, (128, 128)), 0.0)
    i0 = lax.broadcasted_iota(jnp.int32, (KEYS, KEYS), 0)
    i1 = lax.broadcasted_iota(jnp.int32, (KEYS, KEYS), 1)
    m_ref[...] = jnp.where(i0 == i1, 1.0, 0.0).astype(F32)
    for s in range(nsuper):
        following, early = None, None
        for j in range(8):
            following, early = factor16(R, 128 * s + 16 * j, s, j, nt, following, early)
            if 8 * s + j in hooks:
                hooks[8 * s + j]()
        us = R[128 * s : 128 * s + 128, 128 * s + 128 :]
        h, m, l = split3(us)
        right = [jnp.concatenate([h, m], 0), jnp.concatenate([h, l], 0), jnp.concatenate([h, m], 0)]
        for t in range(s + 1, nt):
            c0 = 128 * (t - s - 1)
            lh, lm, ll = split3(jnp.transpose(us[:, c0 : c0 + 128]))
            left = [jnp.concatenate([lh, lh], 1), jnp.concatenate([lm, lh], 1), jnp.concatenate([ll, lm], 1)]
            update = (
                mm(left[0], right[0][:, c0:]) + mm(left[1], right[1][:, c0:]) + mm(left[2], right[2][:, c0:])
            )
            if t < nsuper:
                R[128 * t : 128 * t + 128, 128 * t :] -= update
            else:
                q = 128 * (t - nsuper)
                m_ref[q : q + 128, q:] -= update
    m_ref[128:, :128] = jnp.transpose(m_ref[:128, 128:])
    qh, ql = split2(R[:, n:])
    q2_out[...] = jnp.concatenate([qh, ql], axis=1)

    for half in range(2):

        @pl.when(row == YS * half)
        def _():
            part = pl.ds(PANEL * half, PANEL)
            copy = pltpu.make_async_copy(R.at[part, part], u_out, s_local.at[2])
            copy.start()
            copy.wait()

    await_bytes(wide.at[pl.ds(0, YS - 1)], r_own)
    for step in range(4):
        for way in range(2 if step < 3 else 1):
            await_bytes(wide.at[pl.ds(0, YS - 1)], r_y.at[way, step])

    @pl.when(core != lax.rem(z, 2))
    def _():
        await_bytes(window, r_v)

    @pl.when(col < 2)
    def _():
        await_bytes(crit.at[0, pl.ds(0, XS - 1)], s_x.at[0])

    await_bytes(x_sums.at[pl.ds(0, XS - 1)], s_x.at[1])
    await_bytes(crit.at[0, pl.ds(0, ROWS - 1)], s_r.at[0])
    await_bytes(sums.at[0, pl.ds(0, ROWS - 1)], s_r.at[1])
    await_bytes(crit.at[0], s_p.at[0])
    await_bytes(sums.at[0], s_p.at[1])
    await_bytes(wide.at[pl.ds(0, YS - 1)], s_own)
    for step in range(4):
        wait_z(step, s_z)
        for way in range(2 if step < 3 else 1):
            await_bytes(wide.at[pl.ds(0, YS - 1)], s_y.at[way, step])

    @pl.when(z == col)
    def _():
        await_bytes(window.at[pl.ds(0, YS * XS - 1)], s_w)

    @pl.when(z != col)
    def _():
        await_bytes(window.at[pl.ds(0, YS * XS)], s_w)

    @pl.when(core == lax.rem(z, 2))
    def _():
        await_bytes(window, s_v)


def fused(ridge, keys, shifts):
    dma = pltpu.SemaphoreType.DMA
    vmem = pl.BlockSpec(memory_space=pltpu.VMEM)
    anyspace = pl.BlockSpec(memory_space=pl.ANY)
    return pl.pallas_call(
        fused_kernel,
        out_shape=(
            jax.ShapeDtypeStruct((ROWS, SLAB, WIDE), BF16),
            jax.ShapeDtypeStruct((ROWS, SLAB, WIN), BF16),
            jax.ShapeDtypeStruct((2 * PANEL, 2 * KEYS), BF16),
            jax.ShapeDtypeStruct((KEYS, KEYS), F32),
            jax.ShapeDtypeStruct((8, 128), F32),
            jax.ShapeDtypeStruct((PANEL, PANEL), F32),
        ),
        in_specs=[pl.BlockSpec(memory_space=pltpu.SMEM), vmem, vmem],
        out_specs=(anyspace, anyspace, vmem, vmem, vmem, anyspace),
        scratch_shapes=[
            pltpu.VMEM((2, ROWS, SLAB, PANEL), BF16),
            pltpu.VMEM((2, ROWS, 1, 128), F32),
            pltpu.VMEM((1, 1, 128), F32),
            pltpu.VMEM((XS, 1, 128), F32),
            pltpu.VMEM((2 * PANEL, 2 * PANEL + KEYS), F32),
            dma((3,)), dma((2,)), dma((2,)), dma((2,)), dma((2,)), dma((2,)), dma((2,)), dma, dma,
            dma((2, 4)), dma((2, 4)), dma((2, 4)), dma((2, 4)),
            dma, dma, dma, dma,
        ],
        compiler_params=pltpu.CompilerParams(collective_id=0, has_side_effects=True),
        name="fused",
    )(ridge, keys, shifts)


def output_kernel(
    q2, m, amount_ref, u_hbm, win, wide, pa_out, pb_out, tr_out, fw_out,
    u, kt, pa, pb, tr, fw, in_sem, sems,
):
    row, col = lax.axis_index("row"), lax.axis_index("col")
    z, y = row // YS, lax.rem(row, YS)
    chunks = COL_UNITS // 256
    special = (row == 0) | (row == YS)

    load_u = pltpu.make_async_copy(u_hbm, u, in_sem)

    @pl.when(special)
    def _():
        load_u.start()

    kt[...] = jnp.transpose(win[...].astype(F32)).astype(BF16)
    off = pl.multiple_of(64 * lax.rem(y, 2), 64)
    k_rows = kt[pl.ds(off, ROW_UNITS), :]
    k_rows2 = jnp.concatenate([k_rows, k_rows], axis=1)
    m_parts = jnp.concatenate(split3(m[...]), axis=0)
    th, tl = split2(mm(jnp.concatenate([k_rows, k_rows, k_rows], axis=1), m_parts))
    t2 = jnp.concatenate([th, tl], axis=1)

    copies = []

    def send(src, dst, sem):
        copies.append(pltpu.make_async_copy(src, dst, sems.at[sem]))
        copies[-1].start()

    def trailing_chunk(q):
        lanes = pl.ds(256 * q, 256)
        k = wide[:, 256 * q : 256 * q + 256]
        tr[:, lanes] = mm(t2, jnp.concatenate([k, k], axis=0))

        @pl.when((z == col) & (y * ROW_UNITS < 256 * (q + 1)) & ((y + 1) * ROW_UNITS > 256 * q))
        def _():
            r0 = lax.broadcasted_iota(jnp.int32, (ROW_UNITS, 256), 0)
            r1 = lax.broadcasted_iota(jnp.int32, (ROW_UNITS, 256), 1)
            hit = r1 + (256 * q) == r0 + y * ROW_UNITS
            tr[:, lanes] += jnp.where(hit, amount_ref[0:1, 0:1], 0.0)

        @pl.when(special)
        def _():
            tr[:PANEL, lanes] = jnp.zeros((PANEL, 256), F32)

        if q == 0:

            @pl.when(col < 2)
            def _():
                tr[:, lanes] = jnp.zeros((ROW_UNITS, 256), F32)

        send(tr.at[:, lanes], tr_out.at[:, lanes], 3 + q)

    for q in range(3):
        trailing_chunk(q)

    both = mm_nt(k_rows2, q2[...])
    pa[...] = both[:, :PANEL]
    pb[...] = both[:, PANEL:]

    @pl.when(special)
    def _():
        load_u.wait()
        i0 = lax.broadcasted_iota(jnp.int32, (PANEL, PANEL), 0)
        i1 = lax.broadcasted_iota(jnp.int32, (PANEL, PANEL), 1)
        lower = jnp.where(i0 >= i1, jnp.transpose(u[...]), 0.0)
        pb[:PANEL, :] = lower

        @pl.when(row == 0)
        def _():
            pa[:PANEL, :] = lower
            pb[:PANEL, :] = jnp.zeros((PANEL, PANEL), F32)

    send(pa, pa_out, 0)
    send(pb, pb_out, 1)

    v = wide[:, COL_UNITS:]
    v2 = jnp.concatenate([v, v], axis=0)
    fw[...] = mm(t2, v2)

    @pl.when(special)
    def _():
        start = pl.multiple_of(PANEL * (row // YS), PANEL)
        fw[:PANEL, :] = mm(q2[pl.ds(start, PANEL), :], v2)

    send(fw, fw_out, 2)
    for q in range(3, chunks):
        trailing_chunk(q)
    for copy in copies:
        copy.wait()


def outputs(q2, m, amount, u, win, wide):
    vmem = pl.BlockSpec(memory_space=pltpu.VMEM)
    anyspace = pl.BlockSpec(memory_space=pl.ANY)
    shapes = [(ROW_UNITS, PANEL), (ROW_UNITS, PANEL), (ROW_UNITS, COL_UNITS), (ROW_UNITS, SHIFTS)]
    chunks = COL_UNITS // 256
    return pl.pallas_call(
        output_kernel,
        out_shape=tuple(jax.ShapeDtypeStruct(s, F32) for s in shapes),
        in_specs=[vmem, vmem, vmem, anyspace, vmem, vmem],
        out_specs=(anyspace,) * 4,
        scratch_shapes=[
            pltpu.VMEM((PANEL, PANEL), F32),
            pltpu.VMEM((WIN, KEYS), BF16),
        ]
        + [pltpu.VMEM(s, F32) for s in shapes]
        + [pltpu.SemaphoreType.DMA, pltpu.SemaphoreType.DMA((3 + chunks,))],
        name="outputs",
    )(q2, m, amount, u, win, wide)


def on_device(edit_keys, edit_shifts, ridge_scale):
    wide, window, q2, m, amount, u = fused(ridge_scale, edit_keys, edit_shifts)
    return outputs(q2, m, amount, u, window.reshape(KEYS, WIN), wide.reshape(KEYS, WIDE))


def solution(mesh):
    return jax.shard_map(
        on_device,
        mesh=mesh,
        in_specs=(P("row", "col"), P("row", "col"), P()),
        out_specs=(P("row", None), P("row", None), P("row", "col"), P("row", "col")),
        check_vma=False,
    )
```

```python
import functools

import jax
import jax.numpy as jnp
from jax import lax
from jax.experimental import pallas as pl
from jax.experimental.pallas import tpu as pltpu
from jax.sharding import PartitionSpec as P

F32, BF16 = jnp.float32, jnp.bfloat16
PANEL = 256
ROWS, COLS, YS = 32, 8, 4
ZS = ROWS // YS
SLAB = 8
UNITS = 14336
COL_UNITS = UNITS // COLS
ROW_UNITS = UNITS // ROWS
SHIFTS = 512
WIDE = COL_UNITS + SHIFTS
WIN = 512
KEYS = 256
MESH = pl.DeviceIdType.MESH


def split2(x):
    high = x.astype(BF16)
    return high, (x - high.astype(F32)).astype(BF16)


def split3(x):
    high = x.astype(BF16)
    rest = x - high.astype(F32)
    mid = rest.astype(BF16)
    return high, mid, (rest - mid.astype(F32)).astype(BF16)


def mm(a, b):
    return jnp.dot(a, b, preferred_element_type=F32)


def mm_nt(a, b):
    return lax.dot_general(a, b, (((1,), (1,)), ((), ())), preferred_element_type=F32)


def remote(src, dst, send, recv, row, col):
    return pltpu.make_async_remote_copy(
        src_ref=src, dst_ref=dst, send_sem=send, recv_sem=recv, device_id=(row, col), device_id_type=MESH
    )


def row_bcast(v, k):
    return jnp.broadcast_to(v[k : k + 1, :], (8, v.shape[1]))


def factor16(R, base, s, j, nt, diag_next, early):
    o = 16 * j
    iota = lax.broadcasted_iota(jnp.int32, (8, 128), 0)
    last = j == 7
    ng = 2 if last else 4
    lanes = slice(128 * s, 128 * s + 128)
    T = list(diag_next) if diag_next is not None else [R[base + 8 * g : base + 8 * g + 8, lanes] for g in range(2)]
    for g in range(2, ng):
        T.append(R[base + 8 * g : base + 8 * g + 8, lanes])
    C = [[None] * 4 for _ in range(16)]
    for k in range(16):
        for g in range(k // 8, ng):
            if early is not None and g == 0:
                C[k][g] = early[k]
            else:
                C[k][g] = jnp.broadcast_to(T[g][:, o + k : o + k + 1], (8, 128))
    ahead = None
    Y = {t: [R[base + 8 * g : base + 8 * g + 8, 128 * t : 128 * t + 128] for g in range(2)] for t in range(s + 1, nt)}
    rv = [jnp.zeros((8, 128), F32)] * 2
    for k in range(16):
        gk, kk = k // 8, k % 8
        p = row_bcast(C[k][gk], kk)
        rp = 1.0 / p
        rv[gk] = jnp.where(iota == kk, lax.rsqrt(p), rv[gk])
        M = [None] * 4
        for g in range(gk, ng):
            M[g] = C[k][g] * rp
        for jj in range(k + 1, 16):
            c = row_bcast(C[k][jj // 8], jj % 8)
            for g in range(jj // 8, ng):
                C[jj][g] = C[jj][g] - M[g] * c
        M[gk] = None if kk == 7 else jnp.where(iota > kk, M[gk], 0.0)
        yk = row_bcast(T[gk], kk)
        for g in range(gk, ng):
            if M[g] is not None:
                T[g] = T[g] - M[g] * yk
        for t in range(s + 1, nt):
            yk = row_bcast(Y[t][gk], kk)
            for g in range(gk, 2):
                if M[g] is not None:
                    Y[t][g] = Y[t][g] - M[g] * yk
        if not last:
            if k == 11:
                ahead = [jnp.broadcast_to(T[2][:, o + 16 + q : o + 17 + q], (8, 128)) for q in range(8)]
            elif k > 11:
                ahead = [ahead[q] - M[2] * row_bcast(C[k][2], q) for q in range(8)]
    U = {s: jnp.concatenate([T[0] * rv[0], T[1] * rv[1]], axis=0)}
    for t in range(s + 1, nt):
        U[t] = jnp.concatenate([Y[t][0] * rv[0], Y[t][1] * rv[1]], axis=0)
    for t in range(s, nt):
        R[base : base + 16, 128 * t : 128 * t + 128] = U[t]
    if last:
        return None, None
    zero = jnp.zeros((16, 128), BF16)
    parts = {t: split3(U[t]) for t in range(s, nt)}
    h, m, l = parts[s]
    left = jnp.concatenate([h, h, m, h, l, m, zero, zero], axis=0)
    left = jnp.transpose(left.astype(F32)).astype(BF16)[16 * (j + 1) :, :]
    below = 16 * (7 - j)
    for t in range(s, nt):
        h, m, l = parts[t]
        right = jnp.concatenate([h, m, h, l, h, m, zero, zero], axis=0)
        if t == s:
            if below > 16:
                R[base + 32 : base + 16 + below, lanes] -= mm(left[16:], right)
        else:
            R[base + 16 : base + 16 + below, 128 * t : 128 * t + 128] -= mm(left, right)
    return (T[2], T[3]), ahead


XS = COLS // 2
HALVES = (pl.ds(0, 1152), pl.ds(1152, 1152))


def fused_kernel(
    ridge, keys, shifts, wide, window, q2_out, m_ref, amount_ref, u_out,
    crit, sums, own_sum, x_sums, R,
    s_local, s_x, r_x, s_r, r_r, s_p, r_p, s_own, r_own, s_z, r_z, s_y, r_y, s_w, r_w, s_v, r_v,
):
    row, col = lax.axis_index("row"), lax.axis_index("col")
    z, y = row // YS, lax.rem(row, YS)
    x, core = col // 2, lax.rem(col, 2)
    partner = 2 * x + 1 - core

    def await_bytes(ref, sem):
        pltpu.make_async_copy(ref, ref, sem).wait()

    barrier = pltpu.get_barrier_semaphore()

    def greet(r, c):
        pl.semaphore_signal(barrier, inc=1, device_id=(r, c), device_id_type=MESH)

    def greet_row(i, carry):
        greet(lax.rem(row + i, ROWS), col)
        return carry

    for i in range(1, XS):
        greet(row, lax.rem(col + 2 * i, COLS))
    greet(row, partner)
    lax.fori_loop(1, ROWS, greet_row, 0, unroll=True)

    k32 = keys[...].astype(F32)
    sq = k32 * k32
    part = sq[:, 0:128]
    for t in range(1, COL_UNITS // 128):
        part = part + sq[:, 128 * t : 128 * (t + 1)]
    own_sum[0] = jnp.sum(part, axis=0, keepdims=True)

    local = [
        pltpu.make_async_copy(keys, wide.at[row, :, pl.ds(0, COL_UNITS)], s_local.at[0]),
        pltpu.make_async_copy(shifts, wide.at[row, :, pl.ds(COL_UNITS, SHIFTS)], s_local.at[1]),
    ]
    for copy in local:
        copy.start()

    @pl.when(col < 2)
    def _():
        copy = pltpu.make_async_copy(keys.at[:, pl.ds(0, PANEL)], crit.at[core, row], s_local.at[2])
        copy.start()
        copy.wait()

    @pl.when(z == col)
    def _():
        for yy in range(YS):
            start = yy * ROW_UNITS - 64 * (yy % 2)

            @pl.when(y == yy)
            def _():
                copy = pltpu.make_async_copy(keys.at[:, pl.ds(start, WIN)], window.at[row], s_local.at[2])
                copy.start()
                copy.wait()

    for copy in local:
        copy.wait()
    pl.semaphore_wait(barrier, ROWS + XS - 1)

    up = lax.rem(z + 1, ZS) * YS
    down = lax.rem(z + ZS - 1, ZS) * YS

    def over_y(slot, send, recv):
        for i in range(1, YS):
            ref = wide.at[slot * YS + y]
            remote(ref, ref, send, recv, z * YS + lax.rem(y + i, YS), col).start()

    def step_ref(slot, step, way):
        ref = wide.at[slot * YS + y]
        return ref if step < 3 else ref.at[:, HALVES[way]]

    def round_z(step):
        for way, (source, target) in enumerate(((lax.rem(z + ZS - step, ZS), up), (lax.rem(z + step, ZS), down))):
            ref = step_ref(source, step, way)
            remote(ref, ref, s_z.at[way, step], r_z.at[way, step], target + y, col).start()

    def wait_z(step, sems):
        for way in range(2):
            await_bytes(step_ref(0, step, way), sems.at[way, step])

    def spread_y(step):
        over_y(lax.rem(z + ZS - step - 1, ZS), s_y.at[0, step], r_y.at[0, step])
        if step < 3:
            over_y(lax.rem(z + step + 1, ZS), s_y.at[1, step], r_y.at[1, step])

    @pl.when(col < 2)
    def _():
        for i in range(1, XS):
            remote(
                keys.at[:, pl.ds(0, PANEL)], crit.at[core, row], s_x.at[0], r_x.at[0], row, lax.rem(col + 2 * i, COLS)
            ).start()

    for i in range(1, XS):
        remote(own_sum.at[0], x_sums.at[x], s_x.at[1], r_x.at[1], row, lax.rem(col + 2 * i, COLS)).start()
    x_sums[x] = own_sum[0]
    over_y(z, s_own, r_own)
    round_z(0)

    @pl.when(col >= 2)
    def _():
        await_bytes(crit.at[0, 0], r_x.at[0])

    def send_slab(i, carry):
        remote(crit.at[core, row], crit.at[core, row], s_r.at[0], r_r.at[0], lax.rem(row + i, ROWS), col).start()
        return carry

    def send_sum(i, carry):
        remote(sums.at[core, row], sums.at[core, row], s_r.at[1], r_r.at[1], lax.rem(row + i, ROWS), col).start()
        return carry

    await_bytes(x_sums.at[pl.ds(0, XS - 1)], r_x.at[1])
    sums[core, row] = jnp.sum(x_sums[...], axis=0)
    lax.fori_loop(1, ROWS, send_slab, 0, unroll=True)
    lax.fori_loop(1, ROWS, send_sum, 0, unroll=True)
    wait_z(0, r_z)
    round_z(1)
    await_bytes(crit.at[0, pl.ds(0, ROWS - 1)], r_r.at[0])
    await_bytes(sums.at[0, pl.ds(0, ROWS - 1)], r_r.at[1])

    remote(crit.at[core], crit.at[core], s_p.at[0], r_p.at[0], row, partner).start()
    remote(sums.at[core], sums.at[core], s_p.at[1], r_p.at[1], row, partner).start()

    spread_y(0)
    wait_z(1, r_z)
    round_z(2)
    spread_y(1)

    for yy in range(YS):
        start = yy * ROW_UNITS - 64 * (yy % 2)
        target = col * YS + yy
        for i in range(1, XS):
            remote(
                keys.at[:, pl.ds(start, WIN)], window.at[row], s_w, r_w, target, lax.rem(col + 2 * i, COLS)
            ).start()

        @pl.when(target != row)
        def _():
            remote(keys.at[:, pl.ds(start, WIN)], window.at[row], s_w, r_w, target, col).start()

    def swap_window():
        @pl.when(core == lax.rem(z, 2))
        def _():
            @pl.when(col == z)
            def _():
                await_bytes(window.at[pl.ds(0, ROWS - 1)], r_w)

            @pl.when(col != z)
            def _():
                await_bytes(window, r_w)

            remote(window, window, s_v, r_v, row, partner).start()

    def hook_three():
        wait_z(2, r_z)
        round_z(3)
        spread_y(2)

    def hook_four():
        wait_z(3, r_z)
        spread_y(3)

    hooks = {7: hook_three, 15: hook_four, 23: swap_window}

    await_bytes(crit.at[0], r_p.at[0])
    await_bytes(sums.at[0], r_p.at[1])

    nsuper = 4
    n = 2 * PANEL
    nt = nsuper + 2
    total = jnp.sum(sums[0] + sums[1], axis=0)
    total = jnp.sum(total, axis=1, keepdims=True)
    amount = ridge[0] * total / UNITS
    amount_ref[...] = jnp.broadcast_to(amount, (8, 128))
    first = crit[0].astype(F32).reshape(KEYS, PANEL)
    second = crit[1].astype(F32).reshape(KEYS, PANEL)
    kp32 = jnp.concatenate([first, second], axis=1)
    kp = kp32.astype(BF16)
    kpt = jnp.transpose(kp32)
    R[:, n:] = kpt
    kptb = kpt.astype(BF16)
    i0 = lax.broadcasted_iota(jnp.int32, (128, 128), 0)
    i1 = lax.broadcasted_iota(jnp.int32, (128, 128), 1)
    for s in range(nsuper):
        rows = slice(128 * s, 128 * s + 128)
        R[rows, 128 * s : n] = mm(kptb[rows, :], kp[:, 128 * s :])
        R[rows, rows] += jnp.where(i0 == i1, jnp.broadcast_to(amount, (128, 128)), 0.0)
    i0 = lax.broadcasted_iota(jnp.int32, (KEYS, KEYS), 0)
    i1 = lax.broadcasted_iota(jnp.int32, (KEYS, KEYS), 1)
    m_ref[...] = jnp.where(i0 == i1, 1.0, 0.0).astype(F32)
    for s in range(nsuper):
        following, early = None, None
        for j in range(8):
            following, early = factor16(R, 128 * s + 16 * j, s, j, nt, following, early)
            if 8 * s + j in hooks:
                hooks[8 * s + j]()
        us = R[128 * s : 128 * s + 128, 128 * s + 128 :]
        h, m, l = split3(us)
        right = [jnp.concatenate([h, m], 0), jnp.concatenate([h, l], 0), jnp.concatenate([h, m], 0)]
        for t in range(s + 1, nt):
            c0 = 128 * (t - s - 1)
            lh, lm, ll = split3(jnp.transpose(us[:, c0 : c0 + 128]))
            left = [jnp.concatenate([lh, lh], 1), jnp.concatenate([lm, lh], 1), jnp.concatenate([ll, lm], 1)]
            update = (
                mm(left[0], right[0][:, c0:]) + mm(left[1], right[1][:, c0:]) + mm(left[2], right[2][:, c0:])
            )
            if t < nsuper:
                R[128 * t : 128 * t + 128, 128 * t :] -= update
            else:
                q = 128 * (t - nsuper)
                m_ref[q : q + 128, q:] -= update
    m_ref[128:, :128] = jnp.transpose(m_ref[:128, 128:])
    qh, ql = split2(R[:, n:])
    q2_out[...] = jnp.concatenate([qh, ql], axis=1)

    for half in range(2):

        @pl.when(row == YS * half)
        def _():
            part = pl.ds(PANEL * half, PANEL)
            copy = pltpu.make_async_copy(R.at[part, part], u_out, s_local.at[2])
            copy.start()
            copy.wait()

    await_bytes(wide.at[pl.ds(0, YS - 1)], r_own)
    for step in range(4):
        for way in range(2 if step < 3 else 1):
            await_bytes(wide.at[pl.ds(0, YS - 1)], r_y.at[way, step])

    @pl.when(core != lax.rem(z, 2))
    def _():
        await_bytes(window, r_v)

    @pl.when(col < 2)
    def _():
        await_bytes(crit.at[0, pl.ds(0, XS - 1)], s_x.at[0])

    await_bytes(x_sums.at[pl.ds(0, XS - 1)], s_x.at[1])
    await_bytes(crit.at[0, pl.ds(0, ROWS - 1)], s_r.at[0])
    await_bytes(sums.at[0, pl.ds(0, ROWS - 1)], s_r.at[1])
    await_bytes(crit.at[0], s_p.at[0])
    await_bytes(sums.at[0], s_p.at[1])
    await_bytes(wide.at[pl.ds(0, YS - 1)], s_own)
    for step in range(4):
        wait_z(step, s_z)
        for way in range(2 if step < 3 else 1):
            await_bytes(wide.at[pl.ds(0, YS - 1)], s_y.at[way, step])

    @pl.when(z == col)
    def _():
        await_bytes(window.at[pl.ds(0, YS * XS - 1)], s_w)

    @pl.when(z != col)
    def _():
        await_bytes(window.at[pl.ds(0, YS * XS)], s_w)

    @pl.when(core == lax.rem(z, 2))
    def _():
        await_bytes(window, s_v)


def fused(ridge, keys, shifts):
    dma = pltpu.SemaphoreType.DMA
    vmem = pl.BlockSpec(memory_space=pltpu.VMEM)
    anyspace = pl.BlockSpec(memory_space=pl.ANY)
    return pl.pallas_call(
        fused_kernel,
        out_shape=(
            jax.ShapeDtypeStruct((ROWS, SLAB, WIDE), BF16),
            jax.ShapeDtypeStruct((ROWS, SLAB, WIN), BF16),
            jax.ShapeDtypeStruct((2 * PANEL, 2 * KEYS), BF16),
            jax.ShapeDtypeStruct((KEYS, KEYS), F32),
            jax.ShapeDtypeStruct((8, 128), F32),
            jax.ShapeDtypeStruct((PANEL, PANEL), F32),
        ),
        in_specs=[pl.BlockSpec(memory_space=pltpu.SMEM), vmem, vmem],
        out_specs=(anyspace, anyspace, vmem, vmem, vmem, anyspace),
        scratch_shapes=[
            pltpu.VMEM((2, ROWS, SLAB, PANEL), BF16),
            pltpu.VMEM((2, ROWS, 1, 128), F32),
            pltpu.VMEM((1, 1, 128), F32),
            pltpu.VMEM((XS, 1, 128), F32),
            pltpu.VMEM((2 * PANEL, 2 * PANEL + KEYS), F32),
            dma((3,)), dma((2,)), dma((2,)), dma((2,)), dma((2,)), dma((2,)), dma((2,)), dma, dma,
            dma((2, 4)), dma((2, 4)), dma((2, 4)), dma((2, 4)),
            dma, dma, dma, dma,
        ],
        compiler_params=pltpu.CompilerParams(collective_id=0, has_side_effects=True),
        name="fused",
    )(ridge, keys, shifts)


def output_kernel(
    q2, m, amount_ref, u_hbm, win, wide, pa_out, pb_out, tr_out, fw_out,
    u, kt, pa, pb, tr, fw, in_sem, sems,
):
    row, col = lax.axis_index("row"), lax.axis_index("col")
    z, y = row // YS, lax.rem(row, YS)
    chunks = COL_UNITS // 256
    special = (row == 0) | (row == YS)

    load_u = pltpu.make_async_copy(u_hbm, u, in_sem)

    @pl.when(special)
    def _():
        load_u.start()

    kt[...] = jnp.transpose(win[...].astype(F32)).astype(BF16)
    off = pl.multiple_of(64 * lax.rem(y, 2), 64)
    k_rows = kt[pl.ds(off, ROW_UNITS), :]
    k_rows2 = jnp.concatenate([k_rows, k_rows], axis=1)
    m_parts = jnp.concatenate(split3(m[...]), axis=0)
    th, tl = split2(mm(jnp.concatenate([k_rows, k_rows, k_rows], axis=1), m_parts))
    t2 = jnp.concatenate([th, tl], axis=1)

    copies = []

    def send(src, dst, sem):
        copies.append(pltpu.make_async_copy(src, dst, sems.at[sem]))
        copies[-1].start()

    def trailing_chunk(q):
        lanes = pl.ds(256 * q, 256)
        k = wide[:, 256 * q : 256 * q + 256]
        tr[:, lanes] = mm(t2, jnp.concatenate([k, k], axis=0))

        @pl.when((z == col) & (y * ROW_UNITS < 256 * (q + 1)) & ((y + 1) * ROW_UNITS > 256 * q))
        def _():
            r0 = lax.broadcasted_iota(jnp.int32, (ROW_UNITS, 256), 0)
            r1 = lax.broadcasted_iota(jnp.int32, (ROW_UNITS, 256), 1)
            hit = r1 + (256 * q) == r0 + y * ROW_UNITS
            tr[:, lanes] += jnp.where(hit, amount_ref[0:1, 0:1], 0.0)

        @pl.when(special)
        def _():
            tr[:PANEL, lanes] = jnp.zeros((PANEL, 256), F32)

        if q == 0:

            @pl.when(col < 2)
            def _():
                tr[:, lanes] = jnp.zeros((ROW_UNITS, 256), F32)

        send(tr.at[:, lanes], tr_out.at[:, lanes], 3 + q)

    for q in range(3):
        trailing_chunk(q)

    both = mm_nt(k_rows2, q2[...])
    pa[...] = both[:, :PANEL]
    pb[...] = both[:, PANEL:]

    @pl.when(special)
    def _():
        load_u.wait()
        i0 = lax.broadcasted_iota(jnp.int32, (PANEL, PANEL), 0)
        i1 = lax.broadcasted_iota(jnp.int32, (PANEL, PANEL), 1)
        lower = jnp.where(i0 >= i1, jnp.transpose(u[...]), 0.0)
        pb[:PANEL, :] = lower

        @pl.when(row == 0)
        def _():
            pa[:PANEL, :] = lower
            pb[:PANEL, :] = jnp.zeros((PANEL, PANEL), F32)

    send(pa, pa_out, 0)
    send(pb, pb_out, 1)

    v = wide[:, COL_UNITS:]
    v2 = jnp.concatenate([v, v], axis=0)
    fw[...] = mm(t2, v2)

    @pl.when(special)
    def _():
        start = pl.multiple_of(PANEL * (row // YS), PANEL)
        fw[:PANEL, :] = mm(q2[pl.ds(start, PANEL), :], v2)

    send(fw, fw_out, 2)
    for q in range(3, chunks):
        trailing_chunk(q)
    for copy in copies:
        copy.wait()


def outputs(q2, m, amount, u, win, wide):
    vmem = pl.BlockSpec(memory_space=pltpu.VMEM)
    anyspace = pl.BlockSpec(memory_space=pl.ANY)
    shapes = [(ROW_UNITS, PANEL), (ROW_UNITS, PANEL), (ROW_UNITS, COL_UNITS), (ROW_UNITS, SHIFTS)]
    chunks = COL_UNITS // 256
    return pl.pallas_call(
        output_kernel,
        out_shape=tuple(jax.ShapeDtypeStruct(s, F32) for s in shapes),
        in_specs=[vmem, vmem, vmem, anyspace, vmem, vmem],
        out_specs=(anyspace,) * 4,
        scratch_shapes=[
            pltpu.VMEM((PANEL, PANEL), F32),
            pltpu.VMEM((WIN, KEYS), BF16),
        ]
        + [pltpu.VMEM(s, F32) for s in shapes]
        + [pltpu.SemaphoreType.DMA, pltpu.SemaphoreType.DMA((3 + chunks,))],
        name="outputs",
    )(q2, m, amount, u, win, wide)


def on_device(edit_keys, edit_shifts, ridge_scale):
    wide, window, q2, m, amount, u = fused(ridge_scale, edit_keys, edit_shifts)
    return outputs(q2, m, amount, u, window.reshape(KEYS, WIN), wide.reshape(KEYS, WIDE))


def solution(mesh):
    return jax.shard_map(
        on_device,
        mesh=mesh,
        in_specs=(P("row", "col"), P("row", "col"), P()),
        out_specs=(P("row", None), P("row", None), P("row", "col"), P("row", "col")),
        check_vma=False,
    )
```
